128 devices in a mesh: rows: 8 (over z, core), cols: 16 (over x, y).
Axes of the slice: x: 4, y: 4, z: 4, core: 2. Of those that a mesh axis runs over, the one named last changes fastest.
Arguments:
- density: bfloat16 [6144, 6144], P('rows', 'cols')
- points: float32 [6144, 3, 256], P(('rows', 'cols')), may hold values from -1 to 1
- grid_weights: float32 [6144, 256], P(('rows', 'cols')), may hold values from 0.002 to 0.02
- centres: float32 [3, 6144], replicated, may hold values from -1 to 1
- exponents: float32 [6144], replicated, may hold values from 3 to 12
- sig_blocks: int32 [6144, 4], P(('rows', 'cols')), may hold values from 0 to 47, as said below
- live_count: int32 [128], P(('rows', 'cols')), may hold values from 1 to 48, as said below
Outputs:
- xc_diag: float32 [6144, 768], P('rows', 'cols')
- batch_energy: float32 [6144], P(('rows', 'cols'))
- exc_total: float32 [], replicated
The draws below stay inside these ranges and needn't reach their ends.
Inputs may be any that keep to these rules, and one draw needn't show every extreme that they name: `sig_blocks`: each row holds 4 different blocks in rising order, all among the 48 // 8 blocks of the batch's row group. `live_count`: some device has all 48 slots in use.
All inputs are finite; a program needn't handle non-finite values.
Results may differ from the reference program's by a relative error of at most 0.0005.
Values may be sent and summed in bfloat16 or wider, within the bound.
No kernel may reach another device: no remote copies, remote signals or barrier semaphores. Data moves between devices by JAX's collectives and lax.ppermute only.
A program may use at most 64 MiB of HBM per device.

```python
import math
import jax
import jax.numpy as jnp
from jax import lax

BLOCK = 128
NBLK = 48
NSIG = 4
PTS = 256
BAT_DEV = 48
NBASIS = 6144
BATCHES = 6144
N_ROWS = 8
N_COLS = 16
DEVICES = 128


def draw_density(key, part):
    first, second = jax.random.split(jax.random.fold_in(key, 11), 2)
    scale = 40.0 / (NSIG * BLOCK)
    spread = 1.2 * scale
    raw = jnp.clip(jax.random.normal(first, (NBASIS, NBASIS), jnp.float32), -4.0, 4.0)
    diag = jax.random.uniform(second, (NBASIS,), jnp.float32, 1.0, 3.0)
    sym = (raw + raw.T) * (spread * 0.70710678)
    sym = sym - jnp.diag(jnp.diag(sym))
    full = sym + jnp.diag(diag * scale)
    return full.astype(jnp.bfloat16)


def draw_sig_blocks(key, part):
    span = NBLK // N_ROWS
    scores = jax.random.randint(jax.random.fold_in(key, 23), (BATCHES, span), 0, 1 << 20)
    scores = scores * span + jnp.arange(span, dtype=jnp.int32)[None, :]
    chosen = jnp.sort(jnp.argsort(scores, axis=1)[:, :NSIG].astype(jnp.int32), axis=1)
    group = (jnp.arange(BATCHES, dtype=jnp.int32) // (BAT_DEV * N_COLS))[:, None]
    return (chosen + group * span).astype(jnp.int32)


def draw_live_count(key, part):
    first, second = jax.random.split(jax.random.fold_in(key, 37))
    counts = jax.random.randint(first, (DEVICES,), 1, BAT_DEV + 1)
    full = jax.random.randint(second, (), 0, DEVICES)
    return jnp.where(jnp.arange(DEVICES) == full, BAT_DEV, counts).astype(jnp.int32)


def shard_levels(key, dims, pieces, low, high):
    factor_of, own = 1.0, jax.random.fold_in(key, 6)
    for position, parts in pieces:
        heights = jnp.exp(jax.random.uniform(jax.random.fold_in(own, position), (parts,), jnp.float32, low / len(pieces), high / len(pieces)))
        factor_of = factor_of * jnp.repeat(heights, dims[position] // parts).reshape([-1 if axis == position else 1 for axis in range(len(dims))])
    return factor_of


def setup_inputs(seed: int = 0) -> dict:
    seeds = jax.random.split(jax.random.key(seed), 8)
    density = draw_density(jax.random.fold_in(seeds[7], 71), 0)
    points = jnp.clip(jax.random.uniform(seeds[1], (BATCHES, 3, PTS), jnp.float32, -1.0, 1.0) * shard_levels(seeds[1], (BATCHES, 3, PTS), ((0, 128),), -0.4, 0.0), -1.0, 1.0)
    grid_weights = jnp.clip(jnp.exp(math.log(0.02) - 2.30258502 * jax.random.uniform(seeds[2], (BATCHES, PTS), jnp.float32) ** shard_levels(seeds[2], (BATCHES, PTS), ((0, 128),), -0.2, 0.2)), 0.002, 0.02)
    centres = jnp.clip(jax.random.uniform(seeds[3], (3, NBASIS), jnp.float32, -1.0, 1.0), -1.0, 1.0)
    exponents = jnp.clip(jnp.exp(jax.random.uniform(seeds[4], (NBASIS,), jnp.float32, math.log(3.0), math.log(12.0))), 3.0, 12.0)
    sig_blocks = draw_sig_blocks(jax.random.fold_in(seeds[7], 71), 0)
    live_count = draw_live_count(jax.random.fold_in(seeds[7], 71), 0)
    return {"density": density, "points": points, "grid_weights": grid_weights, "centres": centres, "exponents": exponents, "sig_blocks": sig_blocks, "live_count": live_count}


slater = 0.7386


def evaluate(coords, centre_sel, expo_sel):
    gap_x = coords[0][None, :] - centre_sel[0][:, None]
    gap_y = coords[1][None, :] - centre_sel[1][:, None]
    gap_z = coords[2][None, :] - centre_sel[2][:, None]
    dist = gap_x * gap_x + gap_y * gap_y + gap_z * gap_z
    return jnp.exp(-expo_sel[:, None] * dist).astype(jnp.bfloat16)


def reference(density, points, grid_weights, centres, exponents, sig_blocks, live_count):
    span = NBLK // N_ROWS
    dens4 = density.reshape(NBLK, BLOCK, NBLK, BLOCK)
    width = NSIG * BLOCK
    centre3 = centres.reshape(3, NBLK, BLOCK)
    expo2 = exponents.reshape(NBLK, BLOCK)

    def step(carry, item):
        coords, weight, sig, index = item
        group = index // (BAT_DEV * N_COLS)
        live = ((index % BAT_DEV) < live_count[index // BAT_DEV]).astype(jnp.float32)
        centre_sel = jnp.take(centre3, sig, axis=1).reshape(3, width)
        expo_sel = jnp.take(expo2, sig, axis=0).reshape(width)
        phi = evaluate(coords, centre_sel, expo_sel)
        p_ss = jnp.take(jnp.take(dens4, sig, axis=0), sig, axis=2).reshape(width, width)
        image = jnp.dot(p_ss, phi, preferred_element_type=jnp.float32)
        phif = phi.astype(jnp.float32)
        rho = jnp.maximum(jnp.sum(phif * image, axis=0), 0.0)
        root = jnp.cbrt(rho)
        energy = live * jnp.sum(weight * (-slater) * rho * root)
        scaled = (phif * (weight * (-4.0 / 3.0 * slater) * root)[None, :]).astype(jnp.bfloat16)
        delta = jnp.dot(phi, scaled.T, preferred_element_type=jnp.float32) * live
        delta = delta.reshape(NSIG, BLOCK, NSIG, BLOCK).transpose(0, 2, 1, 3)
        local = (sig - group * span).astype(jnp.int32)
        carry = carry.at[sig[:, None], :, local[None, :], :].add(delta)
        return carry, energy

    start = jnp.zeros((NBLK, BLOCK, span, BLOCK), jnp.float32)
    indices = jnp.arange(BATCHES, dtype=jnp.int32)
    out4, energies = lax.scan(step, start, (points, grid_weights, sig_blocks, indices))
    return out4.reshape(NBASIS, span * BLOCK), energies, jnp.sum(energies)
```

```python
import functools

import jax
import jax.numpy as jnp
from jax import lax
from jax.experimental import pallas as pl
from jax.experimental.pallas import tpu as pltpu
from jax.sharding import Mesh
from jax.sharding import PartitionSpec as P

BLOCK = 128
NBLK = 48
NSIG = 4
PTS = 256
SLOTS = 48
SPAN = 6
OWN = SPAN * BLOCK
NCOLS = 16
PER = SLOTS // NCOLS
STRIP = OWN // NCOLS
COLS = ("cols_0", "cols_1")
ROWS = ("rows_0", "rows_1")
ROWS_COLS = ("rows_0", "rows_1", "cols_0", "cols_1")

slater = 0.7386

VMEM = pl.BlockSpec(memory_space=pltpu.VMEM)
SMEM = pl.BlockSpec(memory_space=pltpu.SMEM)
ANY = pl.BlockSpec(memory_space=pltpu.HBM)
RING = 4


def exchange(blocks):
    return lax.all_to_all(blocks, COLS, split_axis=0, concat_axis=0, tiled=True)


def pack_kernel(me_ref, pts_ref, w_ref, code_ref, out_ref):
    me = me_ref[0]
    code = code_ref[...]

    def one(s, _):
        d = lax.rem(s + me, NCOLS)
        for k in range(PER):
            for c in range(4):
                src = w_ref if c == 3 else pts_ref.at[c]
                row = src[pl.ds(s + NCOLS * k, 1), :]
                for h in range(2):
                    out_ref[d, pl.ds(8 * k + 2 * c + h, 1), :] = row[:, h * 128 : (h + 1) * 128]
        out_ref[d, pl.ds(8 * PER, 8), :] = code
        return 0

    lax.fori_loop(0, NCOLS, one, 0)


def phi_kernel(me_ref, meta_ref, recv_ref, basis_ref, phi_ref, list_ref, ring_s, sem):
    me = me_ref[0]

    def scan(i, n):
        s = lax.rem(me - i + NCOLS, NCOLS)
        for k in range(PER):
            code = meta_ref[i, s + NCOLS * k]
            list_ref[n] = (i * 4 + k) * 4096 + code
            n = n + (code >= 0).astype(jnp.int32)
        return n

    total = lax.fori_loop(0, NCOLS, scan, 0)
    list_ref[63] = total

    def save(n):
        slot = lax.rem(n, RING)
        return pltpu.make_async_copy(ring_s.at[slot], phi_ref.at[n], sem.at[slot])

    def one(n, _):
        @pl.when(n >= RING)
        def _():
            save(n - RING).wait()

        spot = lax.rem(n, RING)
        v = list_ref[n]
        slot = v // 4096
        code = v % 4096
        i = slot // 4
        k = slot % 4
        tile = recv_ref[i, pl.ds(pl.multiple_of(8 * k, 8), 8), :]
        for t in range(NSIG):
            l = (code >> (3 * t)) & 7
            rows = pl.ds(pl.multiple_of(l * BLOCK, BLOCK), BLOCK)
            cx, cy, cz, neg = (basis_ref[q, rows, :] for q in range(4))
            for h in range(2):
                gx = tile[h : h + 1] - cx
                gy = tile[2 + h : 3 + h] - cy
                gz = tile[4 + h : 5 + h] - cz
                dist = gx * gx + gy * gy + gz * gz
                ring_s[spot, t * BLOCK : (t + 1) * BLOCK, h * 128 : (h + 1) * 128] = jnp.exp(
                    neg * dist
                ).astype(jnp.bfloat16)
        save(n).start()
        return 0

    lax.fori_loop(0, total, one, 0)

    def drain(n, _):
        save(n).wait()
        return 0

    lax.fori_loop(jnp.maximum(total - RING, 0), total, drain, 0)


def xc_kernel(list_ref, dens_ref, phi_ref, recv_ref, out_ref, energy_ref, dens_s, acc_s, scaled_s, term_s, ring_s, sem):
    total = list_ref[63]
    for a in range(SPAN):
        for b in range(SPAN):
            dens_s[a * SPAN + b] = dens_ref[
                a * BLOCK : (a + 1) * BLOCK, b * BLOCK : (b + 1) * BLOCK
            ]
    acc_s[...] = jnp.zeros_like(acc_s)
    scaled_s[...] = jnp.zeros_like(scaled_s)
    term_s[...] = jnp.zeros_like(term_s)

    def load(n):
        slot = lax.rem(n, RING)
        return pltpu.make_async_copy(phi_ref.at[n], ring_s.at[slot], sem.at[slot])

    @pl.when(total > 0)
    def _():
        load(0).start()

    @pl.when(total > 1)
    def _():
        load(1).start()

    def locals_of(n):
        code = list_ref[n] % 4096
        return [(code >> (3 * t)) & 7 for t in range(NSIG)]

    def add_delta(n):
        loc = locals_of(n)
        delta = lax.dot_general(
            scaled_s[...],
            ring_s[lax.rem(n, RING)],
            (((1,), (1,)), ((), ())),
            preferred_element_type=jnp.float32,
        )
        for a in range(NSIG):
            rows = pl.ds(pl.multiple_of(loc[a] * BLOCK, BLOCK), BLOCK)
            for b in range(NSIG):
                acc_s[loc[b], rows, :] += delta[
                    a * BLOCK : (a + 1) * BLOCK, b * BLOCK : (b + 1) * BLOCK
                ]

    def one(n, _):
        @pl.when(n + 2 < total)
        def _():
            load(n + 2).start()

        load(n).wait()
        add_delta(jnp.maximum(n - 1, 0))
        loc = locals_of(n)
        slot = list_ref[n] // 4096
        i = slot // 4
        k = slot % 4
        phi = ring_s[lax.rem(n, RING)]
        p_ss = jnp.concatenate(
            [
                jnp.concatenate([dens_s[loc[a] * SPAN + loc[b]] for b in range(NSIG)], axis=1)
                for a in range(NSIG)
            ],
            axis=0,
        )
        image = jnp.dot(p_ss, phi, preferred_element_type=jnp.float32)
        phif = phi.astype(jnp.float32)
        rho = jnp.maximum(jnp.sum(phif * image, axis=0, keepdims=True), 0.0)
        root = jnp.exp2(jnp.log2(rho) * (1.0 / 3.0))
        w8 = recv_ref[i, pl.ds(pl.multiple_of(8 * k, 8), 8), :]
        weight = jnp.concatenate([w8[6:7], w8[7:8]], axis=1)
        term_s[pl.ds(slot, 1), :] = weight * (-slater) * rho * root
        scaled_s[...] = (phif * (weight * (-4.0 / 3.0 * slater) * root)).astype(jnp.bfloat16)
        return 0

    lax.fori_loop(0, total, one, 0)

    @pl.when(total > 0)
    def _():
        add_delta(total - 1)

    for j in range(NCOLS):
        for b in range(SPAN):
            out_ref[j, :, b * BLOCK : (b + 1) * BLOCK] = acc_s[b, j * STRIP : (j + 1) * STRIP, :]
    terms = jnp.sum(term_s[...], axis=1, keepdims=True)
    energy_ref[...] = jnp.broadcast_to(terms, energy_ref.shape)


def shards(density, points, grid_weights, centres, exponents, sig_blocks, live_count):
    group = lax.axis_index(ROWS)
    me = lax.axis_index(COLS)
    me1 = me.reshape(1).astype(jnp.int32)

    strips = exchange(density.reshape(NCOLS, STRIP, density.shape[1]))
    pair = lax.dynamic_slice_in_dim(strips, group * 2, 2, 0)
    strip = jnp.concatenate([pair[0], pair[1]], axis=1)
    dens = exchange(jnp.broadcast_to(strip[None], (NCOLS, STRIP, OWN))).reshape(OWN, OWN)

    local = (sig_blocks.T - group * SPAN).astype(jnp.float32)
    live = (jnp.arange(SLOTS) < live_count[0]).astype(jnp.float32)
    code = jnp.pad(jnp.concatenate([local, live[None]], axis=0), ((0, 3), (0, 128 - SLOTS)))
    packed = pl.pallas_call(
        pack_kernel,
        out_shape=jax.ShapeDtypeStruct((NCOLS, 8 * PER + 8, 128), jnp.float32),
        in_specs=[SMEM, VMEM, VMEM, VMEM],
        out_specs=VMEM,
        name="pack",
    )(me1, points.transpose(1, 0, 2), grid_weights, code)
    recv = exchange(packed)
    tags = recv[:, 8 * PER : 8 * PER + 5, :SLOTS].astype(jnp.int32)
    meta = tags[:, 0] + 8 * tags[:, 1] + 64 * tags[:, 2] + 512 * tags[:, 3]
    meta = jnp.where(tags[:, 4] > 0, meta, -1)

    own = jnp.concatenate(
        [
            lax.dynamic_slice_in_dim(centres, group * OWN, OWN, 1),
            -lax.dynamic_slice_in_dim(exponents, group * OWN, OWN, 0)[None],
        ],
        axis=0,
    )
    basis = jnp.broadcast_to(own[:, :, None], (4, OWN, 128))
    phi, batches = pl.pallas_call(
        phi_kernel,
        out_shape=(
            jax.ShapeDtypeStruct((SLOTS, NSIG * BLOCK, PTS), jnp.bfloat16),
            jax.ShapeDtypeStruct((64,), jnp.int32),
        ),
        in_specs=[SMEM, SMEM, VMEM, VMEM],
        out_specs=(ANY, SMEM),
        scratch_shapes=[
            pltpu.VMEM((RING, NSIG * BLOCK, PTS), jnp.bfloat16),
            pltpu.SemaphoreType.DMA((RING,)),
        ],
        compiler_params=pltpu.CompilerParams(vmem_limit_bytes=56 << 20),
        cost_estimate=pl.CostEstimate(flops=10 * 32 * 512 * 256, transcendentals=32 * 512 * 256, bytes_accessed=16 << 20),
        name="phi",
    )(me1, meta, recv, basis)

    contrib, terms = pl.pallas_call(
        xc_kernel,
        out_shape=(
            jax.ShapeDtypeStruct((NCOLS, STRIP, OWN), jnp.float32),
            jax.ShapeDtypeStruct((NCOLS * 4, 128), jnp.float32),
        ),
        in_specs=[SMEM, VMEM, ANY, VMEM],
        out_specs=(VMEM, VMEM),
        scratch_shapes=[
            pltpu.VMEM((SPAN * SPAN, BLOCK, BLOCK), jnp.bfloat16),
            pltpu.VMEM((SPAN, OWN, BLOCK), jnp.float32),
            pltpu.VMEM((NSIG * BLOCK, PTS), jnp.bfloat16),
            pltpu.VMEM((NCOLS * 4, PTS), jnp.float32),
            pltpu.VMEM((RING, NSIG * BLOCK, PTS), jnp.bfloat16),
            pltpu.SemaphoreType.DMA((RING,)),
        ],
        compiler_params=pltpu.CompilerParams(vmem_limit_bytes=56 << 20),
        cost_estimate=pl.CostEstimate(flops=32 * 4 * 512 * 512 * 256, transcendentals=0, bytes_accessed=16 << 20),
        name="xc",
    )(batches, dens, phi, recv)

    parts = exchange(contrib)
    terms = terms[:, 0].reshape(NCOLS, 4)
    terms = terms.at[:, 3].set(jnp.sum(terms[:, :PER]))
    back = exchange(terms)
    back2 = lax.dynamic_slice_in_dim(jnp.concatenate([back, back], axis=0), me, NCOLS, 0)
    own_energy = back2[:, :PER].T.reshape(SLOTS)
    exc_total = lax.psum(lax.psum(jnp.sum(back[:, 3]), "rows_0"), "rows_1")
    xc_diag = parts.sum(axis=0).T
    return (xc_diag, own_energy, exc_total)


def solution(mesh):
    torus = Mesh(mesh.devices.reshape(4, 2, 4, 4), ("rows_0", "rows_1", "cols_0", "cols_1"))
    return jax.shard_map(
        shards,
        mesh=torus,
        in_specs=(
            P(ROWS, COLS),
            P(ROWS_COLS, None, None),
            P(ROWS_COLS, None),
            P(),
            P(),
            P(ROWS_COLS, None),
            P(ROWS_COLS),
        ),
        out_specs=(P(ROWS, COLS), P(ROWS_COLS), P()),
        check_vma=False,
    )
```

```python
import functools

import jax
import jax.numpy as jnp
from jax import lax
from jax.experimental import pallas as pl
from jax.experimental.pallas import tpu as pltpu
from jax.sharding import Mesh
from jax.sharding import PartitionSpec as P

BLOCK = 128
NBLK = 48
NSIG = 4
PTS = 256
SLOTS = 48
SPAN = 6
OWN = SPAN * BLOCK
NCOLS = 16
PER = SLOTS // NCOLS
STRIP = OWN // NCOLS
COLS = ("cols_0", "cols_1")
ROWS = ("rows_0", "rows_1")
ROWS_COLS = ("rows_0", "rows_1", "cols_0", "cols_1")

slater = 0.7386

VMEM = pl.BlockSpec(memory_space=pltpu.VMEM)
SMEM = pl.BlockSpec(memory_space=pltpu.SMEM)
ANY = pl.BlockSpec(memory_space=pltpu.HBM)
RING = 4
LIMIT = 50
TOP = 32766.0


def exchange(blocks):
    return lax.all_to_all(blocks, COLS, split_axis=0, concat_axis=0, tiled=True)


def pack_kernel(me_ref, dens_ref, pts_ref, w_ref, code_ref, out_ref, tile_s):
    me = me_ref[0]
    code = code_ref[...]

    def one(s, _):
        d = lax.rem(s + me, NCOLS)
        for k in range(PER):
            for c in range(4):
                src = w_ref if c == 3 else pts_ref.at[c]
                row = src[pl.ds(s + NCOLS * k, 1), :]
                for h in range(2):
                    tile_s[d, pl.ds(8 * k + 2 * c + h, 1), :] = row[:, h * 128 : (h + 1) * 128]
        tile_s[d, pl.ds(8 * PER, 8), :] = code
        return 0

    lax.fori_loop(0, NCOLS, one, 0)
    for d in range(NCOLS):
        out_ref[d, :STRIP, :] = dens_ref[d * STRIP : (d + 1) * STRIP, :]
        rest = tile_s[d]
        for q in range(3):
            part = rest.astype(jnp.bfloat16)
            rest = rest - part.astype(jnp.float32)
            out_ref[d, STRIP:, q * 128 : (q + 1) * 128] = part


def phi_kernel(me_ref, meta_ref, recv_ref, basis_ref, phi_ref, list_ref, tile_ref, ring_s, sem):
    me = me_ref[0]
    for i in range(NCOLS):
        hi, mid, lo = (
            recv_ref[i, STRIP:, q * 128 : (q + 1) * 128].astype(jnp.float32) for q in range(3)
        )
        tile_ref[i] = (lo + mid) + hi

    def scan(i, n):
        s = lax.rem(me - i + NCOLS, NCOLS)
        for k in range(PER):
            code = meta_ref[i, s + NCOLS * k]
            list_ref[n] = (i * 4 + k) * 4096 + code
            n = n + (code >= 0).astype(jnp.int32)
        return n

    total = lax.fori_loop(0, NCOLS, scan, 0)
    list_ref[63] = total

    def save(n):
        slot = lax.rem(n, RING)
        return pltpu.make_async_copy(ring_s.at[slot], phi_ref.at[n], sem.at[slot])

    def one(n, _):
        @pl.when(n >= RING)
        def _():
            save(n - RING).wait()

        spot = lax.rem(n, RING)
        v = list_ref[n]
        slot = v // 4096
        code = v % 4096
        i = slot // 4
        k = slot % 4
        tile = tile_ref[i, pl.ds(pl.multiple_of(8 * k, 8), 8), :]
        for t in range(NSIG):
            l = (code >> (3 * t)) & 7
            rows = pl.ds(pl.multiple_of(l * BLOCK, BLOCK), BLOCK)
            cx, cy, cz, neg = (basis_ref[q, rows, :] for q in range(4))
            for h in range(2):
                gx = tile[h : h + 1] - cx
                gy = tile[2 + h : 3 + h] - cy
                gz = tile[4 + h : 5 + h] - cz
                dist = gx * gx + gy * gy + gz * gz
                ring_s[spot, t * BLOCK : (t + 1) * BLOCK, h * 128 : (h + 1) * 128] = jnp.exp(
                    neg * dist
                ).astype(jnp.bfloat16)
        save(n).start()
        return 0

    lax.fori_loop(0, total, one, 0)

    def drain(n, _):
        save(n).wait()
        return 0

    lax.fori_loop(jnp.maximum(total - RING, 0), total, drain, 0)


def xc_kernel(me_ref, list_ref, dens_ref, phi_ref, tile_ref, out_ref, total_ref, dens_s, acc_s, scaled_s, term_s, ring_s, sem):
    total = list_ref[63]
    for a in range(SPAN):
        for b in range(SPAN):
            dens_s[a * SPAN + b] = dens_ref[
                a * BLOCK : (a + 1) * BLOCK, b * BLOCK : (b + 1) * BLOCK
            ]
    acc_s[...] = jnp.zeros_like(acc_s)
    scaled_s[...] = jnp.zeros_like(scaled_s)
    term_s[...] = jnp.zeros_like(term_s)

    def load(n):
        slot = lax.rem(n, RING)
        return pltpu.make_async_copy(phi_ref.at[n], ring_s.at[slot], sem.at[slot])

    @pl.when(total > 0)
    def _():
        load(0).start()

    @pl.when(total > 1)
    def _():
        load(1).start()

    def locals_of(n):
        code = list_ref[n] % 4096
        return [(code >> (3 * t)) & 7 for t in range(NSIG)]

    def add_delta(n):
        loc = locals_of(n)
        delta = lax.dot_general(
            scaled_s[...],
            ring_s[lax.rem(n, RING)],
            (((1,), (1,)), ((), ())),
            preferred_element_type=jnp.float32,
        )
        for a in range(NSIG):
            rows = pl.ds(pl.multiple_of(loc[a] * BLOCK, BLOCK), BLOCK)
            for b in range(NSIG):
                acc_s[loc[b], rows, :] += delta[
                    a * BLOCK : (a + 1) * BLOCK, b * BLOCK : (b + 1) * BLOCK
                ]

    def one(n, _):
        @pl.when(n + 2 < total)
        def _():
            load(n + 2).start()

        load(n).wait()
        add_delta(jnp.maximum(n - 1, 0))
        loc = locals_of(n)
        slot = list_ref[n] // 4096
        i = slot // 4
        k = slot % 4
        phi = ring_s[lax.rem(n, RING)]
        p_ss = jnp.concatenate(
            [
                jnp.concatenate([dens_s[loc[a] * SPAN + loc[b]] for b in range(NSIG)], axis=1)
                for a in range(NSIG)
            ],
            axis=0,
        )
        image = jnp.dot(p_ss, phi, preferred_element_type=jnp.float32)
        phif = phi.astype(jnp.float32)
        rho = jnp.maximum(jnp.sum(phif * image, axis=0, keepdims=True), 0.0)
        root = jnp.exp2(jnp.log2(rho) * (1.0 / 3.0))
        w8 = tile_ref[i, pl.ds(pl.multiple_of(8 * k, 8), 8), :]
        weight = jnp.concatenate([w8[6:7], w8[7:8]], axis=1)
        term_s[pl.ds(slot, 1), :] = weight * (-slater) * rho * root
        scaled_s[...] = (phif * (weight * (-4.0 / 3.0 * slater) * root)).astype(jnp.bfloat16)
        return 0

    lax.fori_loop(0, total, one, 0)

    @pl.when(total > 0)
    def _():
        add_delta(total - 1)

    me = me_ref[0]
    terms = jnp.broadcast_to(jnp.sum(term_s[...], axis=1, keepdims=True), (NCOLS * 4, 128))
    total_ref[...] = jnp.broadcast_to(jnp.sum(terms, axis=0, keepdims=True), total_ref.shape)
    peak = jnp.max(jnp.abs(terms), axis=0, keepdims=True)
    term_code = quarter_octaves(peak)
    terms = terms * (TOP * jnp.exp2(-0.25 * term_code))
    row = lax.broadcasted_iota(jnp.int32, (STRIP, 128), 0)
    lane = lax.broadcasted_iota(jnp.int32, (STRIP, 128), 1)
    for j in range(NCOLS):
        rows = slice(j * STRIP, (j + 1) * STRIP)
        peak = jnp.abs(acc_s[0, rows, :])
        for b in range(1, SPAN):
            peak = jnp.maximum(peak, jnp.abs(acc_s[b, rows, :]))
        code = quarter_octaves(jnp.max(peak, axis=1, keepdims=True))
        scale = TOP * jnp.exp2(-0.25 * code)
        for b in range(SPAN):
            out_ref[j, :, b * BLOCK : (b + 1) * BLOCK] = to_short(acc_s[b, rows, :] * scale)
        s = lax.rem(me - j + NCOLS, NCOLS)
        energy = jnp.zeros((STRIP, 128), jnp.float32)
        for k in range(PER):
            here = terms[4 * j + k : 4 * j + k + 1]
            energy = energy + jnp.where(row == s + NCOLS * k, here, 0.0)
        high = jnp.round(energy)
        low = (energy - high) * (2.0 * TOP)
        extra = jnp.where(lane == 0, high, jnp.where(lane == 1, low, jnp.where(lane == 2, code, term_code)))
        out_ref[j, :, OWN:] = to_short(extra)


def quarter_octaves(peak):
    return jnp.clip(jnp.ceil(4.0 * jnp.log2(peak)), -480.0, 500.0)


def to_short(x):
    return jnp.round(x).astype(jnp.int32).astype(jnp.int16)


def merge_kernel(recv_ref, xc_ref, energy_ref):
    energy = jnp.zeros((STRIP, 128), jnp.float32)
    lane = lax.broadcasted_iota(jnp.int32, (STRIP, 128), 1)
    total = [jnp.zeros((STRIP, 128), jnp.float32) for _ in range(SPAN)]
    for j in range(NCOLS):
        extra = recv_ref[j, :, OWN:].astype(jnp.int32).astype(jnp.float32)
        scale = (1.0 / TOP) * jnp.exp2(0.25 * extra[:, 2:4])
        for b in range(SPAN):
            part = recv_ref[j, :, b * BLOCK : (b + 1) * BLOCK].astype(jnp.int32)
            total[b] = total[b] + part.astype(jnp.float32) * scale[:, :1]
        energy = energy + jnp.where(lane == 0, extra, extra * (0.5 / TOP)) * scale[:, 1:]
    for b in range(SPAN):
        xc_ref[:, b * BLOCK : (b + 1) * BLOCK] = total[b]
    energy_ref[...] = (energy[:, :1] + energy[:, 1:2]) * jnp.ones((1, 128), jnp.float32)


def doubled(value):
    for axis, count in (("rows_1", 2), ("rows_0", 4), ("cols_0", 4), ("cols_1", 4)):
        for other in (1, 3)[: count // 2]:
            value = value + lax.ppermute(value, axis, [(a, a ^ other) for a in range(count)])
    return value


def shards(density, points, grid_weights, centres, exponents, sig_blocks, live_count):
    group = lax.axis_index(ROWS)
    me = lax.axis_index(COLS)
    me1 = me.reshape(1).astype(jnp.int32)

    local = (sig_blocks.T - group * SPAN).astype(jnp.float32)
    live = (jnp.arange(SLOTS) < live_count[0]).astype(jnp.float32)
    code = jnp.pad(jnp.concatenate([local, live[None]], axis=0), ((0, 3), (0, 128 - SLOTS)))
    packed = pl.pallas_call(
        pack_kernel,
        out_shape=jax.ShapeDtypeStruct((NCOLS, STRIP + 32, 384), jnp.bfloat16),
        in_specs=[SMEM, VMEM, VMEM, VMEM, VMEM],
        out_specs=VMEM,
        scratch_shapes=[pltpu.VMEM((NCOLS, 32, 128), jnp.float32)],
        compiler_params=pltpu.CompilerParams(vmem_limit_bytes=16 << 20),
        name="pack",
    )(me1, density, points.transpose(1, 0, 2), grid_weights, code)
    recv = exchange(packed)

    pair = lax.dynamic_slice(recv, (group * 2, 0, 0), (2, STRIP, 384))
    strip = jnp.concatenate([pair[0], pair[1]], axis=1)
    dens = exchange(jnp.broadcast_to(strip[None], (NCOLS, STRIP, OWN))).reshape(OWN, OWN)

    tags = recv[:, STRIP + 24 : STRIP + 29, :SLOTS].astype(jnp.int32)
    meta = tags[:, 0] + 8 * tags[:, 1] + 64 * tags[:, 2] + 512 * tags[:, 3]
    meta = jnp.where(tags[:, 4] > 0, meta, -1)

    own = jnp.concatenate(
        [
            lax.dynamic_slice_in_dim(centres, group * OWN, OWN, 1),
            -lax.dynamic_slice_in_dim(exponents, group * OWN, OWN, 0)[None],
        ],
        axis=0,
    )
    basis = jnp.broadcast_to(own[:, :, None], (4, OWN, 128))
    phi, batches, tiles = pl.pallas_call(
        phi_kernel,
        out_shape=(
            jax.ShapeDtypeStruct((SLOTS, NSIG * BLOCK, PTS), jnp.bfloat16),
            jax.ShapeDtypeStruct((64,), jnp.int32),
            jax.ShapeDtypeStruct((NCOLS, 32, 128), jnp.float32),
        ),
        in_specs=[SMEM, SMEM, VMEM, VMEM],
        out_specs=(ANY, SMEM, VMEM),
        scratch_shapes=[
            pltpu.VMEM((RING, NSIG * BLOCK, PTS), jnp.bfloat16),
            pltpu.SemaphoreType.DMA((RING,)),
        ],
        compiler_params=pltpu.CompilerParams(vmem_limit_bytes=LIMIT << 20),
        cost_estimate=pl.CostEstimate(
            flops=10 * 32 * 512 * 256, transcendentals=32 * 512 * 256, bytes_accessed=16 << 20
        ),
        name="phi",
    )(me1, meta, recv, basis)

    contrib, total = pl.pallas_call(
        xc_kernel,
        out_shape=(
            jax.ShapeDtypeStruct((NCOLS, STRIP, OWN + 128), jnp.int16),
            jax.ShapeDtypeStruct((8, 128), jnp.float32),
        ),
        in_specs=[SMEM, SMEM, VMEM, ANY, VMEM],
        out_specs=(VMEM, VMEM),
        scratch_shapes=[
            pltpu.VMEM((SPAN * SPAN, BLOCK, BLOCK), jnp.bfloat16),
            pltpu.VMEM((SPAN, OWN, BLOCK), jnp.float32),
            pltpu.VMEM((NSIG * BLOCK, PTS), jnp.bfloat16),
            pltpu.VMEM((NCOLS * 4, PTS), jnp.float32),
            pltpu.VMEM((RING, NSIG * BLOCK, PTS), jnp.bfloat16),
            pltpu.SemaphoreType.DMA((RING,)),
        ],
        compiler_params=pltpu.CompilerParams(vmem_limit_bytes=LIMIT << 20),
        cost_estimate=pl.CostEstimate(
            flops=32 * 4 * 512 * 512 * 256, transcendentals=0, bytes_accessed=16 << 20
        ),
        name="xc",
    )(me1, batches, dens, phi, tiles)

    parts = exchange(contrib)
    exc_total = doubled(total)[0, 0]
    xc_rows, energy = pl.pallas_call(
        merge_kernel,
        out_shape=(
            jax.ShapeDtypeStruct((STRIP, OWN), jnp.float32),
            jax.ShapeDtypeStruct((STRIP, 128), jnp.float32),
        ),
        in_specs=[VMEM],
        out_specs=(VMEM, VMEM),
        compiler_params=pltpu.CompilerParams(vmem_limit_bytes=16 << 20),
        name="merge",
    )(parts)
    return (xc_rows.T, energy[:, 0], exc_total)


def solution(mesh):
    torus = Mesh(mesh.devices.reshape(4, 2, 4, 4), ("rows_0", "rows_1", "cols_0", "cols_1"))
    return jax.shard_map(
        shards,
        mesh=torus,
        in_specs=(
            P(ROWS, COLS),
            P(ROWS_COLS, None, None),
            P(ROWS_COLS, None),
            P(),
            P(),
            P(ROWS_COLS, None),
            P(ROWS_COLS),
        ),
        out_specs=(P(ROWS, COLS), P(ROWS_COLS), P()),
        check_vma=False,
    )
```

```python
import jax
import jax.numpy as jnp
from jax import lax
from jax.experimental import pallas as pl
from jax.experimental.pallas import tpu as pltpu
from jax.sharding import Mesh
from jax.sharding import PartitionSpec as P

BLOCK = 128
NSIG = 4
PTS = 256
SLOTS = 48
SPAN = 6
OWN = SPAN * BLOCK
NCOLS = 16
PER = SLOTS // NCOLS
STRIP = OWN // NCOLS
COLS = ("cols_0", "cols_1")
ROWS = ("rows_0", "rows_1")
ROWS_COLS = ("rows_0", "rows_1", "cols_0", "cols_1")

slater = 0.7386

VMEM = pl.BlockSpec(memory_space=pltpu.VMEM)
SMEM = pl.BlockSpec(memory_space=pltpu.SMEM)
ANY = pl.BlockSpec(memory_space=pltpu.HBM)
RING = 16
UNROLL = 4
LIMIT = 50
TOP = 32766.0
EXTRA = 16


def exchange(blocks):
    return lax.all_to_all(blocks, COLS, split_axis=0, concat_axis=0, tiled=True)


def column():
    return 4 * lax.axis_index("cols_0") + lax.axis_index("cols_1")


def pack_kernel(live_ref, dens_ref, pts_ref, w_ref, sig_ref, out_ref, pts_s, w_s, sig_s, tile_s, sem):
    strips = [
        pltpu.make_async_copy(
            dens_ref.at[d * STRIP : (d + 1) * STRIP], out_ref.at[d, :STRIP], sem.at[3 + d]
        )
        for d in range(NCOLS)
    ]
    inputs = [
        pltpu.make_async_copy(src, dst, sem.at[q])
        for q, (src, dst) in enumerate(((pts_ref, pts_s), (w_ref, w_s), (sig_ref, sig_s)))
    ]
    for copy in inputs + strips:
        copy.start()
    for copy in inputs:
        copy.wait()
    me = column()
    group = 2 * lax.axis_index("rows_0") + lax.axis_index("rows_1")
    local = (sig_s[...] - group * SPAN).astype(jnp.float32)
    slots = lax.broadcasted_iota(jnp.int32, (NSIG, SLOTS), 1)
    live = (slots < live_ref[0]).astype(jnp.float32)
    tags = jnp.concatenate([local, live], axis=0)

    def one(s, _):
        d = lax.rem(s + me, NCOLS)
        for k in range(PER):
            for c in range(4):
                src = w_s if c == 3 else pts_s.at[c]
                row = src[pl.ds(s + NCOLS * k, 1), :]
                for h in range(2):
                    tile_s[d, pl.ds(8 * k + 2 * c + h, 1), :] = row[:, h * 128 : (h + 1) * 128]
        tile_s[d, pl.ds(8 * PER, 8), :SLOTS] = tags
        return 0

    tile_s[:, 8 * PER :, :] = jnp.zeros((NCOLS, 8, 128), jnp.float32)
    lax.fori_loop(0, NCOLS, one, 0)
    for d in range(NCOLS):
        rest = tile_s[d]
        for q in range(3):
            part = rest.astype(jnp.bfloat16)
            rest = rest - part.astype(jnp.float32)
            out_ref[d, STRIP:, q * 128 : (q + 1) * 128] = part
    for copy in strips:
        copy.wait()


def phi_kernel(meta_ref, recv_ref, basis_ref, phi_ref, list_ref, tile_ref, ring_s, sem):
    me = column()
    for i in range(NCOLS):
        hi, mid, lo = (
            recv_ref[i, STRIP:, q * 128 : (q + 1) * 128].astype(jnp.float32) for q in range(3)
        )
        tile_ref[i] = (lo + mid) + hi

    def scan(i, n):
        s = lax.rem(me - i + NCOLS, NCOLS)
        for k in range(PER):
            code = meta_ref[i, s + NCOLS * k]
            list_ref[n] = (i * 4 + k) * 4096 + code
            n = n + (code >= 0).astype(jnp.int32)
        return n

    total = lax.fori_loop(0, NCOLS, scan, 0)
    list_ref[63] = total

    def save(n):
        slot = lax.rem(n, RING)
        return pltpu.make_async_copy(ring_s.at[slot], phi_ref.at[n], sem.at[slot])

    def one(n, _):
        @pl.when(n >= RING)
        def _():
            save(n - RING).wait()

        spot = lax.rem(n, RING)
        v = list_ref[n]
        slot = v // 4096
        code = v % 4096
        i = slot // 4
        k = slot % 4
        tile = tile_ref[i, pl.ds(pl.multiple_of(8 * k, 8), 8), :]
        for t in range(NSIG):
            l = (code >> (3 * t)) & 7
            rows = pl.ds(pl.multiple_of(l * BLOCK, BLOCK), BLOCK)
            cx, cy, cz, neg = (basis_ref[q, rows, :] for q in range(4))
            for h in range(2):
                gx = tile[h : h + 1] - cx
                gy = tile[2 + h : 3 + h] - cy
                gz = tile[4 + h : 5 + h] - cz
                dist = gx * gx + gy * gy + gz * gz
                ring_s[spot, t * BLOCK : (t + 1) * BLOCK, h * 128 : (h + 1) * 128] = jnp.exp(
                    neg * dist
                ).astype(jnp.bfloat16)
        save(n).start()
        return 0

    lax.fori_loop(0, total, one, 0)

    def drain(n, _):
        save(n).wait()
        return 0

    lax.fori_loop(jnp.maximum(total - RING, 0), total, drain, 0)


def xc_kernel(
    list_ref, dens_ref, phi_ref, tile_ref, out_ref, total_ref,
    dens_s, acc_s, scaled_s, image_s, factor_s, term_s, ring_s, sem,
):
    total = list_ref[63]

    def load(n):
        slot = lax.rem(n, RING)
        return pltpu.make_async_copy(phi_ref.at[n], ring_s.at[slot], sem.at[slot])

    for u in range(UNROLL):

        @pl.when(u < total)
        def _():
            load(u).start()

    for a in range(SPAN):
        for b in range(SPAN):
            dens_s[a * SPAN + b] = dens_ref[
                a * BLOCK : (a + 1) * BLOCK, b * BLOCK : (b + 1) * BLOCK
            ]
    acc_s[...] = jnp.zeros_like(acc_s)
    scaled_s[...] = jnp.zeros_like(scaled_s)
    image_s[...] = jnp.zeros_like(image_s)
    factor_s[...] = jnp.zeros_like(factor_s)
    term_s[...] = jnp.zeros_like(term_s)

    def locals_of(n):
        code = list_ref[n] % 4096
        return [(code >> (3 * t)) & 7 for t in range(NSIG)]

    def add_delta(n):
        loc = locals_of(n)
        slot = lax.rem(n, RING)
        for h in range(2):
            delta = lax.dot_general(
                scaled_s[...],
                ring_s[slot, h * 2 * BLOCK : (h + 1) * 2 * BLOCK, :],
                (((1,), (1,)), ((), ())),
                preferred_element_type=jnp.float32,
            )
            for a in range(NSIG):
                rows = pl.ds(pl.multiple_of(loc[a] * BLOCK, BLOCK), BLOCK)
                for b in range(2):
                    acc_s[loc[2 * h + b], rows, :] += delta[
                        a * BLOCK : (a + 1) * BLOCK, b * BLOCK : (b + 1) * BLOCK
                    ]

    def scale(n, live):
        factor = jnp.where(live, factor_s[...], 0.0)
        for t in range(NSIG):
            rows = slice(t * BLOCK, (t + 1) * BLOCK)
            phi = ring_s[lax.rem(n, RING), rows, :].astype(jnp.float32)
            scaled_s[rows, :] = (phi * factor).astype(jnp.bfloat16)

    def potential(n):
        slot = list_ref[n] // 4096
        i = slot // 4
        k = slot % 4
        phi = ring_s[lax.rem(n, RING)].astype(jnp.float32)
        rho = jnp.maximum(jnp.sum(phi * image_s[...], axis=0, keepdims=True), 0.0)
        root = jnp.exp2(jnp.log2(rho) * (1.0 / 3.0))
        w8 = tile_ref[i, pl.ds(pl.multiple_of(8 * k, 8), 8), :]
        weight = jnp.concatenate([w8[6:7], w8[7:8]], axis=1)
        term_s[pl.ds(slot, 1), :] = weight * (-slater) * rho * root
        factor_s[...] = weight * (-4.0 / 3.0 * slater) * root

    def image(n):
        loc = locals_of(n)
        p_ss = jnp.concatenate(
            [
                jnp.concatenate([dens_s[loc[a] * SPAN + loc[b]] for b in range(NSIG)], axis=1)
                for a in range(NSIG)
            ],
            axis=0,
        )
        image_s[...] = jnp.dot(p_ss, ring_s[lax.rem(n, RING)], preferred_element_type=jnp.float32)

    def one(m, _):
        first = m * UNROLL
        for u in range(UNROLL):

            @pl.when(first + UNROLL + u < total)
            def _():
                load(first + UNROLL + u).start()

        for u in range(UNROLL):

            @pl.when(first + u < total)
            def _():
                load(first + u).wait()

        for u in range(UNROLL):
            n = first + u
            add_delta(jnp.clip(n - 3, 0, last))
            scale(jnp.clip(n - 2, 0, last), n < total + 2)
            potential(jnp.clip(n - 1, 0, last))
            image(jnp.minimum(n, last))
        return 0

    last = total - 1

    @pl.when(total > 0)
    def _():
        lax.fori_loop(0, (total + 3 + UNROLL - 1) // UNROLL, one, 0)

    me = column()
    terms = jnp.broadcast_to(jnp.sum(term_s[...], axis=1, keepdims=True), (NCOLS * 4, 128))
    total_ref[...] = jnp.broadcast_to(jnp.sum(terms, axis=0, keepdims=True), total_ref.shape)
    peak = jnp.max(jnp.abs(terms), axis=0, keepdims=True)
    term_code = quarter_octaves(peak)
    terms = terms * (TOP * jnp.exp2(-0.25 * term_code))
    row = lax.broadcasted_iota(jnp.int32, (STRIP, 128), 0)
    lane = lax.broadcasted_iota(jnp.int32, (STRIP, 128), 1)
    line = lax.broadcasted_iota(jnp.int32, (EXTRA, 128), 0)
    slot = lane[:1]
    for j in range(NCOLS):
        rows = slice(j * STRIP, (j + 1) * STRIP)
        peak = jnp.abs(acc_s[0, rows, :])
        for b in range(1, SPAN):
            peak = jnp.maximum(peak, jnp.abs(acc_s[b, rows, :]))
        code = quarter_octaves(jnp.max(peak, axis=1, keepdims=True))
        scale = TOP * jnp.exp2(-0.25 * code)
        for b in range(SPAN):
            out_ref[j, b * STRIP : (b + 1) * STRIP, :] = to_short(acc_s[b, rows, :] * scale)
        s = lax.rem(me - j + NCOLS, NCOLS)
        energy = jnp.zeros((1, 128), jnp.float32)
        for k in range(PER):
            here = terms[4 * j + k : 4 * j + k + 1]
            energy = energy + jnp.where(slot == s + NCOLS * k, here, 0.0)
        high = jnp.round(energy)
        low = (energy - high) * (2.0 * TOP)
        codes = jnp.sum(jnp.where(row == lane, code, 0.0), axis=0, keepdims=True)
        extra = jnp.where(line == 0, high, jnp.where(line == 1, low, jnp.where(line == 2, codes, term_code)))
        out_ref[j, SPAN * STRIP :, :] = to_short(extra)


def quarter_octaves(peak):
    return jnp.clip(jnp.ceil(4.0 * jnp.log2(peak)), -480.0, 500.0)


def to_short(x):
    return jnp.round(x).astype(jnp.int32).astype(jnp.int16)


def merge_kernel(recv_ref, xc_ref, energy_ref):
    row = lax.broadcasted_iota(jnp.int32, (STRIP, 128), 0)
    lane = lax.broadcasted_iota(jnp.int32, (STRIP, 128), 1)
    energy = jnp.zeros((1, 128), jnp.float32)
    total = [jnp.zeros((STRIP, 128), jnp.float32) for _ in range(SPAN)]
    for j in range(NCOLS):
        extra = recv_ref[j, SPAN * STRIP :, :].astype(jnp.int32).astype(jnp.float32)
        unit = (1.0 / TOP) * jnp.exp2(0.25 * extra[2:4])
        scale = jnp.sum(jnp.where(row == lane, unit[:1], 0.0), axis=1, keepdims=True)
        for b in range(SPAN):
            part = recv_ref[j, b * STRIP : (b + 1) * STRIP, :].astype(jnp.int32)
            total[b] = total[b] + part.astype(jnp.float32) * scale
        energy = energy + (extra[:1] + extra[1:2] * (0.5 / TOP)) * unit[1:2]
    for b in range(SPAN):
        xc_ref[:, b * BLOCK : (b + 1) * BLOCK] = total[b]
    energy_ref[...] = energy[:, :SLOTS]


def over_all(value):
    left, far, right = (
        lax.ppermute(value, "cols_0", [(a, (a + hop) % 4) for a in range(4)])
        for hop in (1, 2, 3)
    )
    value = (value + far) + (left + right)
    for axis, other in (("rows_1", 1), ("rows_0", 1), ("rows_0", 3), ("cols_1", 1), ("cols_1", 3)):
        moved = lax.ppermute(value, axis, [(a, a ^ other) for a in range(lax.axis_size(axis))])
        value = value + moved
    return value


def shards(density, points, grid_weights, centres, exponents, sig_blocks, live_count):
    group = lax.axis_index(ROWS)

    packed = pl.pallas_call(
        pack_kernel,
        out_shape=jax.ShapeDtypeStruct((NCOLS, STRIP + 32, 384), jnp.bfloat16),
        in_specs=[SMEM, ANY, ANY, ANY, ANY],
        out_specs=VMEM,
        scratch_shapes=[
            pltpu.VMEM((3, SLOTS, PTS), jnp.float32),
            pltpu.VMEM((SLOTS, PTS), jnp.float32),
            pltpu.VMEM((NSIG, SLOTS), jnp.int32),
            pltpu.VMEM((NCOLS, 32, 128), jnp.float32),
            pltpu.SemaphoreType.DMA((3 + NCOLS,)),
        ],
        name="pack",
    )(live_count, density, points.transpose(1, 0, 2), grid_weights, sig_blocks.T)
    recv = exchange(packed)

    pair = lax.dynamic_slice(recv, (group * 2, 0, 0), (2, STRIP, 384))
    strip = jnp.concatenate([pair[0], pair[1]], axis=1)
    dens = exchange(jnp.broadcast_to(strip[None], (NCOLS, STRIP, OWN))).reshape(OWN, OWN)

    tags = recv[:, STRIP + 24 : STRIP + 29, :SLOTS].astype(jnp.int32)
    meta = tags[:, 0] + 8 * tags[:, 1] + 64 * tags[:, 2] + 512 * tags[:, 3]
    meta = jnp.where(tags[:, 4] > 0, meta, -1)

    own = jnp.concatenate(
        [
            lax.dynamic_slice_in_dim(centres, group * OWN, OWN, 1),
            -lax.dynamic_slice_in_dim(exponents, group * OWN, OWN, 0)[None],
        ],
        axis=0,
    )
    basis = jnp.broadcast_to(own[:, :, None], (4, OWN, 128))
    phi, batches, tiles = pl.pallas_call(
        phi_kernel,
        out_shape=(
            jax.ShapeDtypeStruct((SLOTS, NSIG * BLOCK, PTS), jnp.bfloat16),
            jax.ShapeDtypeStruct((64,), jnp.int32),
            jax.ShapeDtypeStruct((NCOLS, 32, 128), jnp.float32),
        ),
        in_specs=[SMEM, VMEM, VMEM],
        out_specs=(ANY, SMEM, VMEM),
        scratch_shapes=[
            pltpu.VMEM((RING, NSIG * BLOCK, PTS), jnp.bfloat16),
            pltpu.SemaphoreType.DMA((RING,)),
        ],
        compiler_params=pltpu.CompilerParams(vmem_limit_bytes=LIMIT << 20),
        cost_estimate=pl.CostEstimate(
            flops=10 * 32 * 512 * 256, transcendentals=32 * 512 * 256, bytes_accessed=16 << 20
        ),
        name="phi",
    )(meta, recv, basis)

    contrib, total = pl.pallas_call(
        xc_kernel,
        out_shape=(
            jax.ShapeDtypeStruct((NCOLS, SPAN * STRIP + EXTRA, BLOCK), jnp.int16),
            jax.ShapeDtypeStruct((8, 128), jnp.float32),
        ),
        in_specs=[SMEM, VMEM, ANY, VMEM],
        out_specs=(VMEM, VMEM),
        scratch_shapes=[
            pltpu.VMEM((SPAN * SPAN, BLOCK, BLOCK), jnp.bfloat16),
            pltpu.VMEM((SPAN, OWN, BLOCK), jnp.float32),
            pltpu.VMEM((NSIG * BLOCK, PTS), jnp.bfloat16),
            pltpu.VMEM((NSIG * BLOCK, PTS), jnp.float32),
            pltpu.VMEM((1, PTS), jnp.float32),
            pltpu.VMEM((NCOLS * 4, PTS), jnp.float32),
            pltpu.VMEM((RING, NSIG * BLOCK, PTS), jnp.bfloat16),
            pltpu.SemaphoreType.DMA((RING,)),
        ],
        compiler_params=pltpu.CompilerParams(vmem_limit_bytes=LIMIT << 20),
        cost_estimate=pl.CostEstimate(
            flops=32 * 4 * 512 * 512 * 256, transcendentals=0, bytes_accessed=16 << 20
        ),
        name="xc",
    )(batches, dens, phi, tiles)

    parts = exchange(contrib)
    exc_total = over_all(total)[0, 0]
    merge = pl.pallas_call(
        merge_kernel,
        out_shape=(
            jax.ShapeDtypeStruct((STRIP, OWN), jnp.float32),
            jax.ShapeDtypeStruct((1, SLOTS), jnp.float32),
        ),
        in_specs=[VMEM],
        out_specs=(VMEM, VMEM),
        compiler_params=pltpu.CompilerParams(vmem_limit_bytes=16 << 20),
        name="merge",
    )
    xc_rows, energy = merge(parts)
    return (xc_rows.T, energy.reshape(SLOTS), exc_total)


def solution(mesh):
    torus = Mesh(mesh.devices.reshape(4, 2, 4, 4), ("rows_0", "rows_1", "cols_0", "cols_1"))
    return jax.shard_map(
        shards,
        mesh=torus,
        in_specs=(
            P(ROWS, COLS),
            P(ROWS_COLS, None, None),
            P(ROWS_COLS, None),
            P(),
            P(),
            P(ROWS_COLS, None),
            P(ROWS_COLS),
        ),
        out_specs=(P(ROWS, COLS), P(ROWS_COLS), P()),
        check_vma=False,
    )
```

```python
import jax
import jax.numpy as jnp
from jax import lax
from jax.experimental import pallas as pl
from jax.experimental.pallas import tpu as pltpu
from jax.sharding import Mesh
from jax.sharding import PartitionSpec as P

BLOCK = 128
NSIG = 4
PTS = 256
SLOTS = 48
SPAN = 6
OWN = SPAN * BLOCK
NCOLS = 16
PER = SLOTS // NCOLS
STRIP = OWN // NCOLS
COLS = ("cols_0", "cols_1")
ROWS = ("rows_0", "rows_1")
ROWS_COLS = ("rows_0", "rows_1", "cols_0", "cols_1")

slater = 0.7386

VMEM = pl.BlockSpec(memory_space=pltpu.VMEM)
SMEM = pl.BlockSpec(memory_space=pltpu.SMEM)
ANY = pl.BlockSpec(memory_space=pltpu.HBM)
RING = 16
UNROLL = 4
LIMIT = 50
TOP = 32766.0
EXTRA = 16


def exchange(blocks):
    return lax.all_to_all(blocks, COLS, split_axis=0, concat_axis=0, tiled=True)


def column():
    return 4 * lax.axis_index("cols_0") + lax.axis_index("cols_1")


def pack_kernel(live_ref, dens_ref, pts_ref, w_ref, sig_ref, out_ref, pts_s, w_s, sig_s, tile_s, sem):
    strips = [
        pltpu.make_async_copy(
            dens_ref.at[d * STRIP : (d + 1) * STRIP], out_ref.at[d, :STRIP], sem.at[3 + d]
        )
        for d in range(NCOLS)
    ]
    inputs = [
        pltpu.make_async_copy(src, dst, sem.at[q])
        for q, (src, dst) in enumerate(((pts_ref, pts_s), (w_ref, w_s), (sig_ref, sig_s)))
    ]
    for copy in inputs + strips:
        copy.start()
    for copy in inputs:
        copy.wait()
    me = column()
    group = 2 * lax.axis_index("rows_0") + lax.axis_index("rows_1")
    local = (sig_s[...] - group * SPAN).astype(jnp.float32)
    slots = lax.broadcasted_iota(jnp.int32, (NSIG, SLOTS), 1)
    live = (slots < live_ref[0]).astype(jnp.float32)
    tags = jnp.concatenate([local, live], axis=0)

    def one(s, _):
        d = lax.rem(s + me, NCOLS)
        for k in range(PER):
            for c in range(4):
                src = w_s if c == 3 else pts_s.at[c]
                row = src[pl.ds(s + NCOLS * k, 1), :]
                for h in range(2):
                    tile_s[d, pl.ds(8 * k + 2 * c + h, 1), :] = row[:, h * 128 : (h + 1) * 128]
        tile_s[d, pl.ds(8 * PER, 8), :SLOTS] = tags
        return 0

    tile_s[:, 8 * PER :, :] = jnp.zeros((NCOLS, 8, 128), jnp.float32)
    lax.fori_loop(0, NCOLS, one, 0)
    for d in range(NCOLS):
        rest = tile_s[d]
        for q in range(3):
            part = rest.astype(jnp.bfloat16)
            rest = rest - part.astype(jnp.float32)
            out_ref[d, STRIP:, q * 128 : (q + 1) * 128] = part
    for copy in strips:
        copy.wait()


def strip_kernel(recv_ref, out_ref):
    first = 2 * (2 * lax.axis_index("rows_0") + lax.axis_index("rows_1"))
    for q in range(2):
        half = recv_ref[first + q, :STRIP, :]
        for d in range(NCOLS):
            out_ref[d, :, q * 384 : (q + 1) * 384] = half


def phi_kernel(meta_ref, recv_ref, basis_ref, phi_ref, list_ref, tile_ref, ring_s, sem):
    me = column()
    for i in range(NCOLS):
        hi, mid, lo = (
            recv_ref[i, STRIP:, q * 128 : (q + 1) * 128].astype(jnp.float32) for q in range(3)
        )
        tile_ref[i] = (lo + mid) + hi

    def scan(i, n):
        s = lax.rem(me - i + NCOLS, NCOLS)
        for k in range(PER):
            code = meta_ref[i, s + NCOLS * k]
            list_ref[n] = (i * 4 + k) * 4096 + code
            n = n + (code >= 0).astype(jnp.int32)
        return n

    total = lax.fori_loop(0, NCOLS, scan, 0)
    list_ref[63] = total

    def save(n):
        slot = lax.rem(n, RING)
        return pltpu.make_async_copy(ring_s.at[slot], phi_ref.at[n], sem.at[slot])

    def one(n, _):
        @pl.when(n >= RING)
        def _():
            save(n - RING).wait()

        spot = lax.rem(n, RING)
        v = list_ref[n]
        slot = v // 4096
        code = v % 4096
        i = slot // 4
        k = slot % 4
        tile = tile_ref[i, pl.ds(pl.multiple_of(8 * k, 8), 8), :]
        for t in range(NSIG):
            l = (code >> (3 * t)) & 7
            rows = pl.ds(pl.multiple_of(l * BLOCK, BLOCK), BLOCK)
            cx, cy, cz, neg = (basis_ref[q, rows, :] for q in range(4))
            for h in range(2):
                gx = tile[h : h + 1] - cx
                gy = tile[2 + h : 3 + h] - cy
                gz = tile[4 + h : 5 + h] - cz
                dist = gx * gx + gy * gy + gz * gz
                ring_s[spot, t * BLOCK : (t + 1) * BLOCK, h * 128 : (h + 1) * 128] = jnp.exp(
                    neg * dist
                ).astype(jnp.bfloat16)
        save(n).start()
        return 0

    lax.fori_loop(0, total, one, 0)

    def drain(n, _):
        save(n).wait()
        return 0

    lax.fori_loop(jnp.maximum(total - RING, 0), total, drain, 0)


def xc_kernel(
    list_ref, dens_ref, phi_ref, tile_ref, out_ref, total_ref,
    dens_s, acc_s, scaled_s, image_s, factor_s, term_s, ring_s, sem,
):
    total = list_ref[63]

    def load(n):
        slot = lax.rem(n, RING)
        return pltpu.make_async_copy(phi_ref.at[n], ring_s.at[slot], sem.at[slot])

    for u in range(UNROLL):

        @pl.when(u < total)
        def _():
            load(u).start()

    for a in range(SPAN):
        for b in range(SPAN):
            dens_s[a * SPAN + b] = dens_ref[
                a * BLOCK : (a + 1) * BLOCK, b * BLOCK : (b + 1) * BLOCK
            ]
    acc_s[...] = jnp.zeros_like(acc_s)
    scaled_s[...] = jnp.zeros_like(scaled_s)
    image_s[...] = jnp.zeros_like(image_s)
    factor_s[...] = jnp.zeros_like(factor_s)
    term_s[...] = jnp.zeros_like(term_s)

    def locals_of(n):
        code = list_ref[n] % 4096
        return [(code >> (3 * t)) & 7 for t in range(NSIG)]

    def add_delta(n):
        loc = locals_of(n)
        slot = lax.rem(n, RING)
        for h in range(2):
            delta = lax.dot_general(
                scaled_s[...],
                ring_s[slot, h * 2 * BLOCK : (h + 1) * 2 * BLOCK, :],
                (((1,), (1,)), ((), ())),
                preferred_element_type=jnp.float32,
            )
            for a in range(NSIG):
                rows = pl.ds(pl.multiple_of(loc[a] * BLOCK, BLOCK), BLOCK)
                for b in range(2):
                    acc_s[loc[2 * h + b], rows, :] += delta[
                        a * BLOCK : (a + 1) * BLOCK, b * BLOCK : (b + 1) * BLOCK
                    ]

    def scale(n, live):
        factor = jnp.where(live, factor_s[...], 0.0)
        for t in range(NSIG):
            rows = slice(t * BLOCK, (t + 1) * BLOCK)
            phi = ring_s[lax.rem(n, RING), rows, :].astype(jnp.float32)
            scaled_s[rows, :] = (phi * factor).astype(jnp.bfloat16)

    def potential(n):
        slot = list_ref[n] // 4096
        i = slot // 4
        k = slot % 4
        phi = ring_s[lax.rem(n, RING)].astype(jnp.float32)
        rho = jnp.maximum(jnp.sum(phi * image_s[...], axis=0, keepdims=True), 0.0)
        root = jnp.exp2(jnp.log2(rho) * (1.0 / 3.0))
        w8 = tile_ref[i, pl.ds(pl.multiple_of(8 * k, 8), 8), :]
        weight = jnp.concatenate([w8[6:7], w8[7:8]], axis=1)
        term_s[pl.ds(slot, 1), :] = weight * (-slater) * rho * root
        factor_s[...] = weight * (-4.0 / 3.0 * slater) * root

    def image(n):
        loc = locals_of(n)
        p_ss = jnp.concatenate(
            [
                jnp.concatenate([dens_s[loc[a] * SPAN + loc[b]] for b in range(NSIG)], axis=1)
                for a in range(NSIG)
            ],
            axis=0,
        )
        image_s[...] = jnp.dot(p_ss, ring_s[lax.rem(n, RING)], preferred_element_type=jnp.float32)

    def one(m, _):
        first = m * UNROLL
        for u in range(UNROLL):

            @pl.when(first + UNROLL + u < total)
            def _():
                load(first + UNROLL + u).start()

        for u in range(UNROLL):

            @pl.when(first + u < total)
            def _():
                load(first + u).wait()

        for u in range(UNROLL):
            n = first + u
            add_delta(jnp.clip(n - 3, 0, last))
            scale(jnp.clip(n - 2, 0, last), n < total + 2)
            potential(jnp.clip(n - 1, 0, last))
            image(jnp.minimum(n, last))
        return 0

    last = total - 1

    @pl.when(total > 0)
    def _():
        lax.fori_loop(0, (total + 3 + UNROLL - 1) // UNROLL, one, 0)

    me = column()
    terms = jnp.broadcast_to(jnp.sum(term_s[...], axis=1, keepdims=True), (NCOLS * 4, 128))
    total_ref[...] = jnp.broadcast_to(jnp.sum(terms, axis=0, keepdims=True), total_ref.shape)
    peak = jnp.max(jnp.abs(terms), axis=0, keepdims=True)
    term_code = quarter_octaves(peak)
    terms = terms * (TOP * jnp.exp2(-0.25 * term_code))
    row = lax.broadcasted_iota(jnp.int32, (STRIP, 128), 0)
    lane = lax.broadcasted_iota(jnp.int32, (STRIP, 128), 1)
    line = lax.broadcasted_iota(jnp.int32, (EXTRA, 128), 0)
    slot = lane[:1]
    for j in range(NCOLS):
        rows = slice(j * STRIP, (j + 1) * STRIP)
        peak = jnp.abs(acc_s[0, rows, :])
        for b in range(1, SPAN):
            peak = jnp.maximum(peak, jnp.abs(acc_s[b, rows, :]))
        code = quarter_octaves(jnp.max(peak, axis=1, keepdims=True))
        scale = TOP * jnp.exp2(-0.25 * code)
        for b in range(SPAN):
            out_ref[j, b * STRIP : (b + 1) * STRIP, :] = to_short(acc_s[b, rows, :] * scale)
        s = lax.rem(me - j + NCOLS, NCOLS)
        energy = jnp.zeros((1, 128), jnp.float32)
        for k in range(PER):
            here = terms[4 * j + k : 4 * j + k + 1]
            energy = energy + jnp.where(slot == s + NCOLS * k, here, 0.0)
        high = jnp.round(energy)
        low = (energy - high) * (2.0 * TOP)
        codes = jnp.sum(jnp.where(row == lane, code, 0.0), axis=0, keepdims=True)
        extra = jnp.where(line == 0, high, jnp.where(line == 1, low, jnp.where(line == 2, codes, term_code)))
        out_ref[j, SPAN * STRIP :, :] = to_short(extra)


def quarter_octaves(peak):
    return jnp.clip(jnp.ceil(4.0 * jnp.log2(peak)), -480.0, 500.0)


def to_short(x):
    return jnp.round(x).astype(jnp.int32).astype(jnp.int16)


def merge_kernel(recv_ref, xc_ref, energy_ref):
    row = lax.broadcasted_iota(jnp.int32, (STRIP, 128), 0)
    lane = lax.broadcasted_iota(jnp.int32, (STRIP, 128), 1)
    energy = jnp.zeros((1, 128), jnp.float32)
    total = [jnp.zeros((STRIP, 128), jnp.float32) for _ in range(SPAN)]
    for j in range(NCOLS):
        extra = recv_ref[j, SPAN * STRIP :, :].astype(jnp.int32).astype(jnp.float32)
        unit = (1.0 / TOP) * jnp.exp2(0.25 * extra[2:4])
        scale = jnp.sum(jnp.where(row == lane, unit[:1], 0.0), axis=1, keepdims=True)
        for b in range(SPAN):
            part = recv_ref[j, b * STRIP : (b + 1) * STRIP, :].astype(jnp.int32)
            total[b] = total[b] + part.astype(jnp.float32) * scale
        energy = energy + (extra[:1] + extra[1:2] * (0.5 / TOP)) * unit[1:2]
    for b in range(SPAN):
        xc_ref[:, b * BLOCK : (b + 1) * BLOCK] = total[b]
    energy_ref[...] = energy[:, :SLOTS]


def over_all(value):
    left, far, right = (
        lax.ppermute(value, "cols_0", [(a, (a + hop) % 4) for a in range(4)])
        for hop in (1, 2, 3)
    )
    value = (value + far) + (left + right)
    for axis, other in (("rows_1", 1), ("rows_0", 1), ("rows_0", 3), ("cols_1", 1), ("cols_1", 3)):
        moved = lax.ppermute(value, axis, [(a, a ^ other) for a in range(lax.axis_size(axis))])
        value = value + moved
    return value


def shards(density, points, grid_weights, centres, exponents, sig_blocks, live_count):
    group = lax.axis_index(ROWS)

    packed = pl.pallas_call(
        pack_kernel,
        out_shape=jax.ShapeDtypeStruct((NCOLS, STRIP + 32, 384), jnp.bfloat16),
        in_specs=[SMEM, ANY, ANY, ANY, ANY],
        out_specs=VMEM,
        scratch_shapes=[
            pltpu.VMEM((3, SLOTS, PTS), jnp.float32),
            pltpu.VMEM((SLOTS, PTS), jnp.float32),
            pltpu.VMEM((NSIG, SLOTS), jnp.int32),
            pltpu.VMEM((NCOLS, 32, 128), jnp.float32),
            pltpu.SemaphoreType.DMA((3 + NCOLS,)),
        ],
        name="pack",
    )(live_count, density, points.transpose(1, 0, 2), grid_weights, sig_blocks.T)
    recv = exchange(packed)

    strips = pl.pallas_call(
        strip_kernel,
        out_shape=jax.ShapeDtypeStruct((NCOLS, STRIP, OWN), jnp.bfloat16),
        in_specs=[VMEM],
        out_specs=VMEM,
        compiler_params=pltpu.CompilerParams(vmem_limit_bytes=16 << 20),
        name="strip",
    )(recv)
    dens = exchange(strips).reshape(OWN, OWN)

    tags = recv[:, STRIP + 24 : STRIP + 29, :SLOTS].astype(jnp.int32)
    meta = tags[:, 0] + 8 * tags[:, 1] + 64 * tags[:, 2] + 512 * tags[:, 3]
    meta = jnp.where(tags[:, 4] > 0, meta, -1)

    own = jnp.concatenate(
        [
            lax.dynamic_slice_in_dim(centres, group * OWN, OWN, 1),
            -lax.dynamic_slice_in_dim(exponents, group * OWN, OWN, 0)[None],
        ],
        axis=0,
    )
    basis = jnp.broadcast_to(own[:, :, None], (4, OWN, 128))
    phi, batches, tiles = pl.pallas_call(
        phi_kernel,
        out_shape=(
            jax.ShapeDtypeStruct((SLOTS, NSIG * BLOCK, PTS), jnp.bfloat16),
            jax.ShapeDtypeStruct((64,), jnp.int32),
            jax.ShapeDtypeStruct((NCOLS, 32, 128), jnp.float32),
        ),
        in_specs=[SMEM, VMEM, VMEM],
        out_specs=(ANY, SMEM, VMEM),
        scratch_shapes=[
            pltpu.VMEM((RING, NSIG * BLOCK, PTS), jnp.bfloat16),
            pltpu.SemaphoreType.DMA((RING,)),
        ],
        compiler_params=pltpu.CompilerParams(vmem_limit_bytes=LIMIT << 20),
        cost_estimate=pl.CostEstimate(
            flops=10 * 32 * 512 * 256, transcendentals=32 * 512 * 256, bytes_accessed=16 << 20
        ),
        name="phi",
    )(meta, recv, basis)

    contrib, total = pl.pallas_call(
        xc_kernel,
        out_shape=(
            jax.ShapeDtypeStruct((NCOLS, SPAN * STRIP + EXTRA, BLOCK), jnp.int16),
            jax.ShapeDtypeStruct((8, 128), jnp.float32),
        ),
        in_specs=[SMEM, VMEM, ANY, VMEM],
        out_specs=(VMEM, VMEM),
        scratch_shapes=[
            pltpu.VMEM((SPAN * SPAN, BLOCK, BLOCK), jnp.bfloat16),
            pltpu.VMEM((SPAN, OWN, BLOCK), jnp.float32),
            pltpu.VMEM((NSIG * BLOCK, PTS), jnp.bfloat16),
            pltpu.VMEM((NSIG * BLOCK, PTS), jnp.float32),
            pltpu.VMEM((1, PTS), jnp.float32),
            pltpu.VMEM((NCOLS * 4, PTS), jnp.float32),
            pltpu.VMEM((RING, NSIG * BLOCK, PTS), jnp.bfloat16),
            pltpu.SemaphoreType.DMA((RING,)),
        ],
        compiler_params=pltpu.CompilerParams(vmem_limit_bytes=LIMIT << 20),
        cost_estimate=pl.CostEstimate(
            flops=32 * 4 * 512 * 512 * 256, transcendentals=0, bytes_accessed=16 << 20
        ),
        name="xc",
    )(batches, dens, phi, tiles)

    parts = exchange(contrib)
    exc_total = over_all(total)[0, 0]
    merge = pl.pallas_call(
        merge_kernel,
        out_shape=(
            jax.ShapeDtypeStruct((STRIP, OWN), jnp.float32),
            jax.ShapeDtypeStruct((1, SLOTS), jnp.float32),
        ),
        in_specs=[VMEM],
        out_specs=(VMEM, VMEM),
        compiler_params=pltpu.CompilerParams(vmem_limit_bytes=16 << 20),
        name="merge",
    )
    xc_rows, energy = merge(parts)
    return (xc_rows.T, energy.reshape(SLOTS), exc_total)


def solution(mesh):
    torus = Mesh(mesh.devices.reshape(4, 2, 4, 4), ("rows_0", "rows_1", "cols_0", "cols_1"))
    return jax.shard_map(
        shards,
        mesh=torus,
        in_specs=(
            P(ROWS, COLS),
            P(ROWS_COLS, None, None),
            P(ROWS_COLS, None),
            P(),
            P(),
            P(ROWS_COLS, None),
            P(ROWS_COLS),
        ),
        out_specs=(P(ROWS, COLS), P(ROWS_COLS), P()),
        check_vma=False,
    )
```

```python
import jax
import jax.numpy as jnp
from jax import lax
from jax.experimental import pallas as pl
from jax.experimental.pallas import tpu as pltpu
from jax.sharding import Mesh
from jax.sharding import PartitionSpec as P

BLOCK = 128
NSIG = 4
PTS = 256
SLOTS = 48
SPAN = 6
OWN = SPAN * BLOCK
NCOLS = 16
PER = SLOTS // NCOLS
STRIP = OWN // NCOLS
COLS = ("cols_0", "cols_1")
ROWS = ("rows_0", "rows_1")
ROWS_COLS = ("rows_0", "rows_1", "cols_0", "cols_1")

slater = 0.7386

VMEM = pl.BlockSpec(memory_space=pltpu.VMEM)
SMEM = pl.BlockSpec(memory_space=pltpu.SMEM)
ANY = pl.BlockSpec(memory_space=pltpu.HBM)
RING = 16
UNROLL = 4
LIMIT = 50
TOP = 32766.0
EXTRA = 16


def exchange(blocks):
    return lax.all_to_all(blocks, COLS, split_axis=0, concat_axis=0, tiled=True)


def column():
    return 4 * lax.axis_index("cols_0") + lax.axis_index("cols_1")


def pack_kernel(live_ref, dens_ref, pts_ref, w_ref, sig_ref, out_ref, pts_s, w_s, sig_s, tile_s, sem):
    strips = [
        pltpu.make_async_copy(
            dens_ref.at[d * STRIP : (d + 1) * STRIP], out_ref.at[d, :STRIP], sem.at[3 + d]
        )
        for d in range(NCOLS)
    ]
    inputs = [
        pltpu.make_async_copy(src, dst, sem.at[q])
        for q, (src, dst) in enumerate(((pts_ref, pts_s), (w_ref, w_s), (sig_ref, sig_s)))
    ]
    for copy in inputs + strips:
        copy.start()
    for copy in inputs:
        copy.wait()
    me = column()
    group = 2 * lax.axis_index("rows_0") + lax.axis_index("rows_1")
    local = (sig_s[...] - group * SPAN).astype(jnp.float32)
    slots = lax.broadcasted_iota(jnp.int32, (NSIG, SLOTS), 1)
    live = (slots < live_ref[0]).astype(jnp.float32)
    tags = jnp.concatenate([local, live], axis=0)

    def one(s, _):
        d = lax.rem(s + me, NCOLS)
        for k in range(PER):
            for c in range(4):
                src = w_s if c == 3 else pts_s.at[c]
                row = src[pl.ds(s + NCOLS * k, 1), :]
                for h in range(2):
                    tile_s[d, pl.ds(8 * k + 2 * c + h, 1), :] = row[:, h * 128 : (h + 1) * 128]
        tile_s[d, pl.ds(8 * PER, 8), :SLOTS] = tags
        return 0

    tile_s[:, 8 * PER :, :] = jnp.zeros((NCOLS, 8, 128), jnp.float32)
    lax.fori_loop(0, NCOLS, one, 0)
    for d in range(NCOLS):
        rest = tile_s[d]
        for q in range(3):
            part = rest.astype(jnp.bfloat16)
            rest = rest - part.astype(jnp.float32)
            out_ref[d, STRIP:, q * 128 : (q + 1) * 128] = part
    for copy in strips:
        copy.wait()


def strip_kernel(recv_ref, out_ref):
    first = 2 * (2 * lax.axis_index("rows_0") + lax.axis_index("rows_1"))
    for q in range(2):
        half = recv_ref[first + q, :STRIP, :]
        for d in range(NCOLS):
            out_ref[d, :, q * 384 : (q + 1) * 384] = half


def phi_kernel(meta_ref, recv_ref, basis_ref, phi_ref, list_ref, tile_ref, ring_s, sem):
    me = column()
    for i in range(NCOLS):
        hi, mid, lo = (
            recv_ref[i, STRIP:, q * 128 : (q + 1) * 128].astype(jnp.float32) for q in range(3)
        )
        tile_ref[i] = (lo + mid) + hi

    def scan(i, n):
        s = lax.rem(me - i + NCOLS, NCOLS)
        for k in range(PER):
            code = meta_ref[i, s + NCOLS * k]
            list_ref[n] = (i * 4 + k) * 4096 + code
            n = n + (code >= 0).astype(jnp.int32)
        return n

    total = lax.fori_loop(0, NCOLS, scan, 0)
    list_ref[63] = total

    def save(n):
        slot = lax.rem(n, RING)
        return pltpu.make_async_copy(ring_s.at[slot], phi_ref.at[n], sem.at[slot])

    def one(n, _):
        @pl.when(n >= RING)
        def _():
            save(n - RING).wait()

        spot = lax.rem(n, RING)
        v = list_ref[n]
        slot = v // 4096
        code = v % 4096
        i = slot // 4
        k = slot % 4
        tile = tile_ref[i, pl.ds(pl.multiple_of(8 * k, 8), 8), :]
        for t in range(NSIG):
            l = (code >> (3 * t)) & 7
            rows = pl.ds(pl.multiple_of(l * BLOCK, BLOCK), BLOCK)
            cx, cy, cz, neg = (basis_ref[q, rows, :] for q in range(4))
            for h in range(2):
                gx = tile[h : h + 1] - cx
                gy = tile[2 + h : 3 + h] - cy
                gz = tile[4 + h : 5 + h] - cz
                dist = gx * gx + gy * gy + gz * gz
                ring_s[spot, t * BLOCK : (t + 1) * BLOCK, h * 128 : (h + 1) * 128] = jnp.exp(
                    neg * dist
                ).astype(jnp.bfloat16)
        save(n).start()
        return 0

    lax.fori_loop(0, total, one, 0)

    def drain(n, _):
        save(n).wait()
        return 0

    lax.fori_loop(jnp.maximum(total - RING, 0), total, drain, 0)


def xc_kernel(
    list_ref, dens_ref, phi_ref, tile_ref, out_ref,
    dens_s, acc_s, scaled_s, image_s, factor_s, term_s, ring_s, sem,
):
    total = list_ref[63]

    def load(n):
        slot = lax.rem(n, RING)
        return pltpu.make_async_copy(phi_ref.at[n], ring_s.at[slot], sem.at[slot])

    for u in range(UNROLL):

        @pl.when(u < total)
        def _():
            load(u).start()

    for a in range(SPAN):
        for b in range(SPAN):
            dens_s[a * SPAN + b] = dens_ref[
                a * BLOCK : (a + 1) * BLOCK, b * BLOCK : (b + 1) * BLOCK
            ]
    acc_s[...] = jnp.zeros_like(acc_s)
    scaled_s[...] = jnp.zeros_like(scaled_s)
    image_s[...] = jnp.zeros_like(image_s)
    factor_s[...] = jnp.zeros_like(factor_s)
    term_s[...] = jnp.zeros_like(term_s)

    def locals_of(n):
        code = list_ref[n] % 4096
        return [(code >> (3 * t)) & 7 for t in range(NSIG)]

    def add_delta(n):
        loc = locals_of(n)
        slot = lax.rem(n, RING)
        for h in range(2):
            delta = lax.dot_general(
                scaled_s[...],
                ring_s[slot, h * 2 * BLOCK : (h + 1) * 2 * BLOCK, :],
                (((1,), (1,)), ((), ())),
                preferred_element_type=jnp.float32,
            )
            for a in range(NSIG):
                rows = pl.ds(pl.multiple_of(loc[a] * BLOCK, BLOCK), BLOCK)
                for b in range(2):
                    acc_s[loc[2 * h + b], rows, :] += delta[
                        a * BLOCK : (a + 1) * BLOCK, b * BLOCK : (b + 1) * BLOCK
                    ]

    def scale(n, live):
        factor = jnp.where(live, factor_s[...], 0.0)
        for t in range(NSIG):
            rows = slice(t * BLOCK, (t + 1) * BLOCK)
            phi = ring_s[lax.rem(n, RING), rows, :].astype(jnp.float32)
            scaled_s[rows, :] = (phi * factor).astype(jnp.bfloat16)

    def potential(n):
        slot = list_ref[n] // 4096
        i = slot // 4
        k = slot % 4
        phi = ring_s[lax.rem(n, RING)].astype(jnp.float32)
        rho = jnp.maximum(jnp.sum(phi * image_s[...], axis=0, keepdims=True), 0.0)
        root = jnp.exp2(jnp.log2(rho) * (1.0 / 3.0))
        w8 = tile_ref[i, pl.ds(pl.multiple_of(8 * k, 8), 8), :]
        weight = jnp.concatenate([w8[6:7], w8[7:8]], axis=1)
        term_s[pl.ds(slot, 1), :] = weight * (-slater) * rho * root
        factor_s[...] = weight * (-4.0 / 3.0 * slater) * root

    def image(n):
        loc = locals_of(n)
        p_ss = jnp.concatenate(
            [
                jnp.concatenate([dens_s[loc[a] * SPAN + loc[b]] for b in range(NSIG)], axis=1)
                for a in range(NSIG)
            ],
            axis=0,
        )
        image_s[...] = jnp.dot(p_ss, ring_s[lax.rem(n, RING)], preferred_element_type=jnp.float32)

    def one(m, _):
        first = m * UNROLL
        for u in range(UNROLL):

            @pl.when(first + UNROLL + u < total)
            def _():
                load(first + UNROLL + u).start()

        for u in range(UNROLL):

            @pl.when(first + u < total)
            def _():
                load(first + u).wait()

        for u in range(UNROLL):
            n = first + u
            add_delta(jnp.clip(n - 3, 0, last))
            scale(jnp.clip(n - 2, 0, last), n < total + 2)
            potential(jnp.clip(n - 1, 0, last))
            image(jnp.minimum(n, last))
        return 0

    last = total - 1

    @pl.when(total > 0)
    def _():
        lax.fori_loop(0, (total + 3 + UNROLL - 1) // UNROLL, one, 0)

    me = column()
    terms = jnp.broadcast_to(jnp.sum(term_s[...], axis=1, keepdims=True), (NCOLS * 4, 128))
    whole = jnp.sum(terms, axis=0, keepdims=True)
    whole_code = quarter_octaves(jnp.abs(whole))
    whole = whole * (TOP * jnp.exp2(-0.25 * whole_code))
    whole_high = jnp.round(whole)
    whole_low = (whole - whole_high) * (2.0 * TOP)
    peak = jnp.max(jnp.abs(terms), axis=0, keepdims=True)
    term_code = quarter_octaves(peak)
    terms = terms * (TOP * jnp.exp2(-0.25 * term_code))
    row = lax.broadcasted_iota(jnp.int32, (STRIP, 128), 0)
    lane = lax.broadcasted_iota(jnp.int32, (STRIP, 128), 1)
    line = lax.broadcasted_iota(jnp.int32, (EXTRA, 128), 0)
    slot = lane[:1]
    for j in range(NCOLS):
        rows = slice(j * STRIP, (j + 1) * STRIP)
        peak = jnp.abs(acc_s[0, rows, :])
        for b in range(1, SPAN):
            peak = jnp.maximum(peak, jnp.abs(acc_s[b, rows, :]))
        code = quarter_octaves(jnp.max(peak, axis=1, keepdims=True))
        scale = TOP * jnp.exp2(-0.25 * code)
        for b in range(SPAN):
            out_ref[j, b * STRIP : (b + 1) * STRIP, :] = to_short(acc_s[b, rows, :] * scale)
        s = lax.rem(me - j + NCOLS, NCOLS)
        energy = jnp.zeros((1, 128), jnp.float32)
        for k in range(PER):
            here = terms[4 * j + k : 4 * j + k + 1]
            energy = energy + jnp.where(slot == s + NCOLS * k, here, 0.0)
        high = jnp.round(energy)
        low = (energy - high) * (2.0 * TOP)
        codes = jnp.sum(jnp.where(row == lane, code, 0.0), axis=0, keepdims=True)
        extra = jnp.zeros((EXTRA, 128), jnp.float32)
        lines = (high, low, codes, term_code, whole_high, whole_low, whole_code)
        for q, values in enumerate(lines):
            extra = jnp.where(line == q, values, extra)
        out_ref[j, SPAN * STRIP :, :] = to_short(extra)


def quarter_octaves(peak):
    return jnp.clip(jnp.ceil(4.0 * jnp.log2(peak)), -480.0, 500.0)


def to_short(x):
    return jnp.round(x).astype(jnp.int32).astype(jnp.int16)


def merge_kernel(recv_ref, xc_ref, energy_ref, total_ref):
    row = lax.broadcasted_iota(jnp.int32, (STRIP, 128), 0)
    lane = lax.broadcasted_iota(jnp.int32, (STRIP, 128), 1)
    energy = whole = jnp.zeros((1, 128), jnp.float32)
    total = [jnp.zeros((STRIP, 128), jnp.float32) for _ in range(SPAN)]
    for j in range(NCOLS):
        extra = recv_ref[j, SPAN * STRIP :, :].astype(jnp.int32).astype(jnp.float32)
        unit = (1.0 / TOP) * jnp.exp2(0.25 * extra[:8])
        scale = jnp.sum(jnp.where(row == lane, unit[2:3], 0.0), axis=1, keepdims=True)
        for b in range(SPAN):
            part = recv_ref[j, b * STRIP : (b + 1) * STRIP, :].astype(jnp.int32)
            total[b] = total[b] + part.astype(jnp.float32) * scale
        energy = energy + (extra[:1] + extra[1:2] * (0.5 / TOP)) * unit[3:4]
        whole = whole + (extra[4:5] + extra[5:6] * (0.5 / TOP)) * unit[6:7]
    for b in range(SPAN):
        xc_ref[:, b * BLOCK : (b + 1) * BLOCK] = total[b]
    energy_ref[...] = energy[:, :SLOTS]
    total_ref[...] = jnp.broadcast_to(whole, total_ref.shape)


def over_rows(value):
    for axis, other in (("rows_1", 1), ("rows_0", 1), ("rows_0", 3)):
        pairs = [(a, a ^ other) for a in range(lax.axis_size(axis))]
        value = value + lax.ppermute(value, axis, pairs)
    return value


def shards(density, points, grid_weights, centres, exponents, sig_blocks, live_count):
    group = lax.axis_index(ROWS)

    packed = pl.pallas_call(
        pack_kernel,
        out_shape=jax.ShapeDtypeStruct((NCOLS, STRIP + 32, 384), jnp.bfloat16),
        in_specs=[SMEM, ANY, ANY, ANY, ANY],
        out_specs=VMEM,
        scratch_shapes=[
            pltpu.VMEM((3, SLOTS, PTS), jnp.float32),
            pltpu.VMEM((SLOTS, PTS), jnp.float32),
            pltpu.VMEM((NSIG, SLOTS), jnp.int32),
            pltpu.VMEM((NCOLS, 32, 128), jnp.float32),
            pltpu.SemaphoreType.DMA((3 + NCOLS,)),
        ],
        name="pack",
    )(live_count, density, points.transpose(1, 0, 2), grid_weights, sig_blocks.T)
    recv = exchange(packed)

    strips = pl.pallas_call(
        strip_kernel,
        out_shape=jax.ShapeDtypeStruct((NCOLS, STRIP, OWN), jnp.bfloat16),
        in_specs=[VMEM],
        out_specs=VMEM,
        compiler_params=pltpu.CompilerParams(vmem_limit_bytes=16 << 20),
        name="strip",
    )(recv)
    dens = exchange(strips).reshape(OWN, OWN)

    tags = recv[:, STRIP + 24 : STRIP + 29, :SLOTS].astype(jnp.int32)
    meta = tags[:, 0] + 8 * tags[:, 1] + 64 * tags[:, 2] + 512 * tags[:, 3]
    meta = jnp.where(tags[:, 4] > 0, meta, -1)

    own = jnp.concatenate(
        [
            lax.dynamic_slice_in_dim(centres, group * OWN, OWN, 1),
            -lax.dynamic_slice_in_dim(exponents, group * OWN, OWN, 0)[None],
        ],
        axis=0,
    )
    basis = jnp.broadcast_to(own[:, :, None], (4, OWN, 128))
    phi, batches, tiles = pl.pallas_call(
        phi_kernel,
        out_shape=(
            jax.ShapeDtypeStruct((SLOTS, NSIG * BLOCK, PTS), jnp.bfloat16),
            jax.ShapeDtypeStruct((64,), jnp.int32),
            jax.ShapeDtypeStruct((NCOLS, 32, 128), jnp.float32),
        ),
        in_specs=[SMEM, VMEM, VMEM],
        out_specs=(ANY, SMEM, VMEM),
        scratch_shapes=[
            pltpu.VMEM((RING, NSIG * BLOCK, PTS), jnp.bfloat16),
            pltpu.SemaphoreType.DMA((RING,)),
        ],
        compiler_params=pltpu.CompilerParams(vmem_limit_bytes=LIMIT << 20),
        cost_estimate=pl.CostEstimate(
            flops=10 * 32 * 512 * 256, transcendentals=32 * 512 * 256, bytes_accessed=16 << 20
        ),
        name="phi",
    )(meta, recv, basis)

    contrib = pl.pallas_call(
        xc_kernel,
        out_shape=jax.ShapeDtypeStruct((NCOLS, SPAN * STRIP + EXTRA, BLOCK), jnp.int16),
        in_specs=[SMEM, VMEM, ANY, VMEM],
        out_specs=VMEM,
        scratch_shapes=[
            pltpu.VMEM((SPAN * SPAN, BLOCK, BLOCK), jnp.bfloat16),
            pltpu.VMEM((SPAN, OWN, BLOCK), jnp.float32),
            pltpu.VMEM((NSIG * BLOCK, PTS), jnp.bfloat16),
            pltpu.VMEM((NSIG * BLOCK, PTS), jnp.float32),
            pltpu.VMEM((1, PTS), jnp.float32),
            pltpu.VMEM((NCOLS * 4, PTS), jnp.float32),
            pltpu.VMEM((RING, NSIG * BLOCK, PTS), jnp.bfloat16),
            pltpu.SemaphoreType.DMA((RING,)),
        ],
        compiler_params=pltpu.CompilerParams(vmem_limit_bytes=LIMIT << 20),
        cost_estimate=pl.CostEstimate(
            flops=32 * 4 * 512 * 512 * 256, transcendentals=0, bytes_accessed=16 << 20
        ),
        name="xc",
    )(batches, dens, phi, tiles)

    parts = exchange(contrib)
    merge = pl.pallas_call(
        merge_kernel,
        out_shape=(
            jax.ShapeDtypeStruct((STRIP, OWN), jnp.float32),
            jax.ShapeDtypeStruct((1, SLOTS), jnp.float32),
            jax.ShapeDtypeStruct((8, 128), jnp.float32),
        ),
        in_specs=[VMEM],
        out_specs=(VMEM, VMEM, VMEM),
        compiler_params=pltpu.CompilerParams(vmem_limit_bytes=16 << 20),
        name="merge",
    )
    xc_rows, energy, total = merge(parts)
    exc_total = over_rows(total)[0, 0]
    return (xc_rows.T, energy.reshape(SLOTS), exc_total)


def solution(mesh):
    torus = Mesh(mesh.devices.reshape(4, 2, 4, 4), ("rows_0", "rows_1", "cols_0", "cols_1"))
    return jax.shard_map(
        shards,
        mesh=torus,
        in_specs=(
            P(ROWS, COLS),
            P(ROWS_COLS, None, None),
            P(ROWS_COLS, None),
            P(),
            P(),
            P(ROWS_COLS, None),
            P(ROWS_COLS),
        ),
        out_specs=(P(ROWS, COLS), P(ROWS_COLS), P()),
        check_vma=False,
    )
```

```python
import jax
import jax.numpy as jnp
from jax import lax
from jax.experimental import pallas as pl
from jax.experimental.pallas import tpu as pltpu
from jax.sharding import Mesh
from jax.sharding import PartitionSpec as P

BLOCK = 128
NSIG = 4
PTS = 256
SLOTS = 48
SPAN = 6
OWN = SPAN * BLOCK
NCOLS = 16
PER = SLOTS // NCOLS
STRIP = OWN // NCOLS
COLS = ("cols_0", "cols_1")
ROWS = ("rows_0", "rows_1")
ROWS_COLS = ("rows_0", "rows_1", "cols_0", "cols_1")

slater = 0.7386

VMEM = pl.BlockSpec(memory_space=pltpu.VMEM)
SMEM = pl.BlockSpec(memory_space=pltpu.SMEM)
ANY = pl.BlockSpec(memory_space=pltpu.HBM)
RING = 16
UNROLL = 4
LIMIT = 50
TOP = 32766.0
EXTRA = 16


def exchange(blocks):
    return lax.all_to_all(blocks, COLS, split_axis=0, concat_axis=0, tiled=True)


def column():
    return 4 * lax.axis_index("cols_0") + lax.axis_index("cols_1")


def pack_kernel(live_ref, dens_ref, pts_ref, w_ref, sig_ref, send_ref, pts_s, w_s, sig_s, tile_s, out_ref, sem):
    strips = [
        pltpu.make_async_copy(
            dens_ref.at[d * STRIP : (d + 1) * STRIP], out_ref.at[d, :STRIP], sem.at[3 + d]
        )
        for d in range(NCOLS)
    ]
    inputs = [
        pltpu.make_async_copy(src, dst, sem.at[q])
        for q, (src, dst) in enumerate(((pts_ref, pts_s), (w_ref, w_s), (sig_ref, sig_s)))
    ]
    for copy in inputs + strips:
        copy.start()
    for copy in inputs:
        copy.wait()
    me = column()
    group = 2 * lax.axis_index("rows_0") + lax.axis_index("rows_1")
    local = (sig_s[...] - group * SPAN).astype(jnp.float32)
    slots = lax.broadcasted_iota(jnp.int32, (NSIG, SLOTS), 1)
    live = (slots < live_ref[0]).astype(jnp.float32)
    tags = jnp.concatenate([local, live], axis=0)

    def one(s, _):
        d = lax.rem(s + me, NCOLS)
        for k in range(PER):
            for c in range(4):
                src = w_s if c == 3 else pts_s.at[c]
                row = src[pl.ds(s + NCOLS * k, 1), :]
                for h in range(2):
                    tile_s[d, pl.ds(8 * k + 2 * c + h, 1), :] = row[:, h * 128 : (h + 1) * 128]
        tile_s[d, pl.ds(8 * PER, 8), :SLOTS] = tags
        return 0

    tile_s[:, 8 * PER :, :] = jnp.zeros((NCOLS, 8, 128), jnp.float32)
    lax.fori_loop(0, NCOLS, one, 0)
    for copy in strips:
        copy.wait()
    outs = [
        pltpu.make_async_copy(out_ref.at[:, rows], send_ref.at[:, rows], sem.at[q])
        for q, rows in enumerate((slice(0, STRIP), slice(STRIP, STRIP + 32)))
    ]
    outs[0].start()
    for d in range(NCOLS):
        rest = tile_s[d]
        for q in range(3):
            part = rest.astype(jnp.bfloat16)
            rest = rest - part.astype(jnp.float32)
            out_ref[d, STRIP:, q * 128 : (q + 1) * 128] = part
    outs[1].start()
    for copy in outs:
        copy.wait()


def strip_kernel(recv_ref, out_ref):
    first = 2 * (2 * lax.axis_index("rows_0") + lax.axis_index("rows_1"))
    for q in range(2):
        half = recv_ref[first + q, :STRIP, :]
        for d in range(NCOLS):
            out_ref[d, :, q * 384 : (q + 1) * 384] = half


def phi_kernel(meta_ref, recv_ref, basis_ref, phi_ref, list_ref, tile_ref, ring_s, sem):
    me = column()
    for i in range(NCOLS):
        hi, mid, lo = (
            recv_ref[i, STRIP:, q * 128 : (q + 1) * 128].astype(jnp.float32) for q in range(3)
        )
        tile_ref[i] = (lo + mid) + hi

    def scan(i, n):
        s = lax.rem(me - i + NCOLS, NCOLS)
        for k in range(PER):
            code = meta_ref[i, s + NCOLS * k]
            list_ref[n] = (i * 4 + k) * 4096 + code
            n = n + (code >= 0).astype(jnp.int32)
        return n

    total = lax.fori_loop(0, NCOLS, scan, 0)
    list_ref[63] = total

    def save(n):
        slot = lax.rem(n, RING)
        return pltpu.make_async_copy(ring_s.at[slot], phi_ref.at[n], sem.at[slot])

    def one(n, _):
        @pl.when(n >= RING)
        def _():
            save(n - RING).wait()

        spot = lax.rem(n, RING)
        v = list_ref[n]
        slot = v // 4096
        code = v % 4096
        i = slot // 4
        k = slot % 4
        tile = tile_ref[i, pl.ds(pl.multiple_of(8 * k, 8), 8), :]
        for t in range(NSIG):
            l = (code >> (3 * t)) & 7
            rows = pl.ds(pl.multiple_of(l * BLOCK, BLOCK), BLOCK)
            cx, cy, cz, neg = (basis_ref[q, rows, :] for q in range(4))
            for h in range(2):
                gx = tile[h : h + 1] - cx
                gy = tile[2 + h : 3 + h] - cy
                gz = tile[4 + h : 5 + h] - cz
                dist = gx * gx + gy * gy + gz * gz
                ring_s[spot, t * BLOCK : (t + 1) * BLOCK, h * 128 : (h + 1) * 128] = jnp.exp(
                    neg * dist
                ).astype(jnp.bfloat16)
        save(n).start()
        return 0

    lax.fori_loop(0, total, one, 0)

    def drain(n, _):
        save(n).wait()
        return 0

    lax.fori_loop(jnp.maximum(total - RING, 0), total, drain, 0)


def xc_kernel(
    list_ref, dens_ref, phi_ref, tile_ref, out_ref, total_ref,
    dens_s, acc_s, scaled_s, image_s, factor_s, term_s, ring_s, sem,
):
    total = list_ref[63]

    def load(n):
        slot = lax.rem(n, RING)
        return pltpu.make_async_copy(phi_ref.at[n], ring_s.at[slot], sem.at[slot])

    for u in range(UNROLL):

        @pl.when(u < total)
        def _():
            load(u).start()

    for a in range(SPAN):
        for b in range(SPAN):
            dens_s[a * SPAN + b] = dens_ref[
                a * BLOCK : (a + 1) * BLOCK, b * BLOCK : (b + 1) * BLOCK
            ]
    acc_s[...] = jnp.zeros_like(acc_s)
    scaled_s[...] = jnp.zeros_like(scaled_s)
    image_s[...] = jnp.zeros_like(image_s)
    factor_s[...] = jnp.zeros_like(factor_s)
    term_s[...] = jnp.zeros_like(term_s)

    def locals_of(n):
        code = list_ref[n] % 4096
        return [(code >> (3 * t)) & 7 for t in range(NSIG)]

    def add_delta(n):
        loc = locals_of(n)
        slot = lax.rem(n, RING)
        for h in range(2):
            delta = lax.dot_general(
                scaled_s[...],
                ring_s[slot, h * 2 * BLOCK : (h + 1) * 2 * BLOCK, :],
                (((1,), (1,)), ((), ())),
                preferred_element_type=jnp.float32,
            )
            for a in range(NSIG):
                rows = pl.ds(pl.multiple_of(loc[a] * BLOCK, BLOCK), BLOCK)
                for b in range(2):
                    acc_s[loc[2 * h + b], rows, :] += delta[
                        a * BLOCK : (a + 1) * BLOCK, b * BLOCK : (b + 1) * BLOCK
                    ]

    def scale(n, live):
        factor = jnp.where(live, factor_s[...], 0.0)
        for t in range(NSIG):
            rows = slice(t * BLOCK, (t + 1) * BLOCK)
            phi = ring_s[lax.rem(n, RING), rows, :].astype(jnp.float32)
            scaled_s[rows, :] = (phi * factor).astype(jnp.bfloat16)

    def potential(n):
        slot = list_ref[n] // 4096
        i = slot // 4
        k = slot % 4
        phi = ring_s[lax.rem(n, RING)].astype(jnp.float32)
        rho = jnp.maximum(jnp.sum(phi * image_s[...], axis=0, keepdims=True), 0.0)
        root = jnp.exp2(jnp.log2(rho) * (1.0 / 3.0))
        w8 = tile_ref[i, pl.ds(pl.multiple_of(8 * k, 8), 8), :]
        weight = jnp.concatenate([w8[6:7], w8[7:8]], axis=1)
        term_s[pl.ds(slot, 1), :] = weight * (-slater) * rho * root
        factor_s[...] = weight * (-4.0 / 3.0 * slater) * root

    def image(n):
        loc = locals_of(n)
        p_ss = jnp.concatenate(
            [
                jnp.concatenate([dens_s[loc[a] * SPAN + loc[b]] for b in range(NSIG)], axis=1)
                for a in range(NSIG)
            ],
            axis=0,
        )
        image_s[...] = jnp.dot(p_ss, ring_s[lax.rem(n, RING)], preferred_element_type=jnp.float32)

    def one(m, _):
        first = m * UNROLL
        for u in range(UNROLL):

            @pl.when(first + UNROLL + u < total)
            def _():
                load(first + UNROLL + u).start()

        for u in range(UNROLL):

            @pl.when(first + u < total)
            def _():
                load(first + u).wait()

        for u in range(UNROLL):
            n = first + u
            add_delta(jnp.clip(n - 3, 0, last))
            scale(jnp.clip(n - 2, 0, last), n < total + 2)
            potential(jnp.clip(n - 1, 0, last))
            image(jnp.minimum(n, last))
        return 0

    last = total - 1

    @pl.when(total > 0)
    def _():
        lax.fori_loop(0, (total + 3 + UNROLL - 1) // UNROLL, one, 0)

    me = column()
    terms = jnp.broadcast_to(jnp.sum(term_s[...], axis=1, keepdims=True), (NCOLS * 4, 128))
    total_ref[...] = jnp.broadcast_to(jnp.sum(terms, axis=0, keepdims=True), total_ref.shape)
    peak = jnp.max(jnp.abs(terms), axis=0, keepdims=True)
    term_code = quarter_octaves(peak)
    terms = terms * (TOP * jnp.exp2(-0.25 * term_code))
    row = lax.broadcasted_iota(jnp.int32, (STRIP, 128), 0)
    lane = lax.broadcasted_iota(jnp.int32, (STRIP, 128), 1)
    line = lax.broadcasted_iota(jnp.int32, (EXTRA, 128), 0)
    slot = lane[:1]
    for j in range(NCOLS):
        rows = slice(j * STRIP, (j + 1) * STRIP)
        peak = jnp.abs(acc_s[0, rows, :])
        for b in range(1, SPAN):
            peak = jnp.maximum(peak, jnp.abs(acc_s[b, rows, :]))
        code = quarter_octaves(jnp.max(peak, axis=1, keepdims=True))
        scale = TOP * jnp.exp2(-0.25 * code)
        for b in range(SPAN):
            out_ref[j, b * STRIP : (b + 1) * STRIP, :] = to_short(acc_s[b, rows, :] * scale)
        s = lax.rem(me - j + NCOLS, NCOLS)
        energy = jnp.zeros((1, 128), jnp.float32)
        for k in range(PER):
            here = terms[4 * j + k : 4 * j + k + 1]
            energy = energy + jnp.where(slot == s + NCOLS * k, here, 0.0)
        high = jnp.round(energy)
        low = (energy - high) * (2.0 * TOP)
        codes = jnp.sum(jnp.where(row == lane, code, 0.0), axis=0, keepdims=True)
        extra = jnp.where(line == 0, high, jnp.where(line == 1, low, jnp.where(line == 2, codes, term_code)))
        out_ref[j, SPAN * STRIP :, :] = to_short(extra)


def quarter_octaves(peak):
    return jnp.clip(jnp.ceil(4.0 * jnp.log2(peak)), -480.0, 500.0)


def to_short(x):
    return jnp.round(x).astype(jnp.int32).astype(jnp.int16)


def merge_kernel(recv_ref, xc_ref, energy_ref):
    row = lax.broadcasted_iota(jnp.int32, (STRIP, 128), 0)
    lane = lax.broadcasted_iota(jnp.int32, (STRIP, 128), 1)
    energy = jnp.zeros((1, 128), jnp.float32)
    total = [jnp.zeros((STRIP, 128), jnp.float32) for _ in range(SPAN)]
    for j in range(NCOLS):
        extra = recv_ref[j, SPAN * STRIP :, :].astype(jnp.int32).astype(jnp.float32)
        unit = (1.0 / TOP) * jnp.exp2(0.25 * extra[2:4])
        scale = jnp.sum(jnp.where(row == lane, unit[:1], 0.0), axis=1, keepdims=True)
        for b in range(SPAN):
            part = recv_ref[j, b * STRIP : (b + 1) * STRIP, :].astype(jnp.int32)
            total[b] = total[b] + part.astype(jnp.float32) * scale
        energy = energy + (extra[:1] + extra[1:2] * (0.5 / TOP)) * unit[1:2]
    for b in range(SPAN):
        xc_ref[:, b * BLOCK : (b + 1) * BLOCK] = total[b]
    energy_ref[...] = energy[:, :SLOTS]


def over_all(value):
    left, far, right = (
        lax.ppermute(value, "cols_0", [(a, (a + hop) % 4) for a in range(4)])
        for hop in (1, 2, 3)
    )
    value = (value + far) + (left + right)
    for axis, other in (("rows_1", 1), ("rows_0", 1), ("rows_0", 3), ("cols_1", 1), ("cols_1", 3)):
        moved = lax.ppermute(value, axis, [(a, a ^ other) for a in range(lax.axis_size(axis))])
        value = value + moved
    return value


def shards(density, points, grid_weights, centres, exponents, sig_blocks, live_count):
    group = lax.axis_index(ROWS)

    packed = pl.pallas_call(
        pack_kernel,
        out_shape=jax.ShapeDtypeStruct((NCOLS, STRIP + 32, 384), jnp.bfloat16),
        in_specs=[SMEM, ANY, ANY, ANY, ANY],
        out_specs=ANY,
        scratch_shapes=[
            pltpu.VMEM((3, SLOTS, PTS), jnp.float32),
            pltpu.VMEM((SLOTS, PTS), jnp.float32),
            pltpu.VMEM((NSIG, SLOTS), jnp.int32),
            pltpu.VMEM((NCOLS, 32, 128), jnp.float32),
            pltpu.VMEM((NCOLS, STRIP + 32, 384), jnp.bfloat16),
            pltpu.SemaphoreType.DMA((3 + NCOLS,)),
        ],
        name="pack",
    )(live_count, density, points.transpose(1, 0, 2), grid_weights, sig_blocks.T)
    recv = exchange(packed)

    strips = pl.pallas_call(
        strip_kernel,
        out_shape=jax.ShapeDtypeStruct((NCOLS, STRIP, OWN), jnp.bfloat16),
        in_specs=[VMEM],
        out_specs=VMEM,
        compiler_params=pltpu.CompilerParams(vmem_limit_bytes=16 << 20),
        name="strip",
    )(recv)
    dens = exchange(strips).reshape(OWN, OWN)

    tags = recv[:, STRIP + 24 : STRIP + 29, :SLOTS].astype(jnp.int32)
    meta = tags[:, 0] + 8 * tags[:, 1] + 64 * tags[:, 2] + 512 * tags[:, 3]
    meta = jnp.where(tags[:, 4] > 0, meta, -1)

    own = jnp.concatenate(
        [
            lax.dynamic_slice_in_dim(centres, group * OWN, OWN, 1),
            -lax.dynamic_slice_in_dim(exponents, group * OWN, OWN, 0)[None],
        ],
        axis=0,
    )
    basis = jnp.broadcast_to(own[:, :, None], (4, OWN, 128))
    phi, batches, tiles = pl.pallas_call(
        phi_kernel,
        out_shape=(
            jax.ShapeDtypeStruct((SLOTS, NSIG * BLOCK, PTS), jnp.bfloat16),
            jax.ShapeDtypeStruct((64,), jnp.int32),
            jax.ShapeDtypeStruct((NCOLS, 32, 128), jnp.float32),
        ),
        in_specs=[SMEM, VMEM, VMEM],
        out_specs=(ANY, SMEM, VMEM),
        scratch_shapes=[
            pltpu.VMEM((RING, NSIG * BLOCK, PTS), jnp.bfloat16),
            pltpu.SemaphoreType.DMA((RING,)),
        ],
        compiler_params=pltpu.CompilerParams(vmem_limit_bytes=LIMIT << 20),
        cost_estimate=pl.CostEstimate(
            flops=10 * 32 * 512 * 256, transcendentals=32 * 512 * 256, bytes_accessed=16 << 20
        ),
        name="phi",
    )(meta, recv, basis)

    contrib, total = pl.pallas_call(
        xc_kernel,
        out_shape=(
            jax.ShapeDtypeStruct((NCOLS, SPAN * STRIP + EXTRA, BLOCK), jnp.int16),
            jax.ShapeDtypeStruct((8, 128), jnp.float32),
        ),
        in_specs=[SMEM, VMEM, ANY, VMEM],
        out_specs=(VMEM, VMEM),
        scratch_shapes=[
            pltpu.VMEM((SPAN * SPAN, BLOCK, BLOCK), jnp.bfloat16),
            pltpu.VMEM((SPAN, OWN, BLOCK), jnp.float32),
            pltpu.VMEM((NSIG * BLOCK, PTS), jnp.bfloat16),
            pltpu.VMEM((NSIG * BLOCK, PTS), jnp.float32),
            pltpu.VMEM((1, PTS), jnp.float32),
            pltpu.VMEM((NCOLS * 4, PTS), jnp.float32),
            pltpu.VMEM((RING, NSIG * BLOCK, PTS), jnp.bfloat16),
            pltpu.SemaphoreType.DMA((RING,)),
        ],
        compiler_params=pltpu.CompilerParams(vmem_limit_bytes=LIMIT << 20),
        cost_estimate=pl.CostEstimate(
            flops=32 * 4 * 512 * 512 * 256, transcendentals=0, bytes_accessed=16 << 20
        ),
        name="xc",
    )(batches, dens, phi, tiles)

    parts = exchange(contrib)
    exc_total = over_all(total)[0, 0]
    merge = pl.pallas_call(
        merge_kernel,
        out_shape=(
            jax.ShapeDtypeStruct((STRIP, OWN), jnp.float32),
            jax.ShapeDtypeStruct((1, SLOTS), jnp.float32),
        ),
        in_specs=[VMEM],
        out_specs=(VMEM, VMEM),
        compiler_params=pltpu.CompilerParams(vmem_limit_bytes=16 << 20),
        name="merge",
    )
    xc_rows, energy = merge(parts)
    return (xc_rows.T, energy.reshape(SLOTS), exc_total)


def solution(mesh):
    torus = Mesh(mesh.devices.reshape(4, 2, 4, 4), ("rows_0", "rows_1", "cols_0", "cols_1"))
    return jax.shard_map(
        shards,
        mesh=torus,
        in_specs=(
            P(ROWS, COLS),
            P(ROWS_COLS, None, None),
            P(ROWS_COLS, None),
            P(),
            P(),
            P(ROWS_COLS, None),
            P(ROWS_COLS),
        ),
        out_specs=(P(ROWS, COLS), P(ROWS_COLS), P()),
        check_vma=False,
    )
```
